256 devices in a mesh: il: 16 (over y, x), xl: 16 (over z, core).
Axes of the slice: x: 4, y: 4, z: 8, core: 2. Of those that a mesh axis runs over, the one named last changes fastest.
Arguments:
- patches: bfloat16 [16, 192, 128, 768], P('il', 'xl'), may hold values from -9 to 9
- out_cot: bfloat16 [16, 192, 128, 768], P('il', 'xl'), may hold values from -6 to 6
- vis_count: int32 [16, 192], P('il', 'xl'), may hold values from 0 to 128, as said below
- w_qkv: bfloat16 [768, 1152], P(('il', 'xl')), may hold values from -1.5 to 1.5
- w_out: bfloat16 [768, 384], P(('il', 'xl')), may hold values from -0.3125 to 0.3125
- ln_gain: float32 [768], replicated, may hold values from 0.1 to 1.9
Outputs:
- enc_out: bfloat16 [16, 192, 128, 768], P('il', 'xl')
- grad_in: bfloat16 [16, 192, 128, 768], P('il', 'xl')
- grad_wqkv: float32 [768, 1152], P(('il', 'xl'))
- grad_wout: float32 [768, 384], P(('il', 'xl'))
The draws below stay inside these ranges and needn't reach their ends.
Inputs may be any that keep to these rules, and one draw needn't show every extreme that they name: `vis_count`: A block with count 0 holds no data. On each inline row of tiles exactly 96 blocks have data; one device holds 0 to 12 of them, and some device of each row holds 12.
All inputs are finite; a program needn't handle non-finite values.
Results may differ from the reference program's by a relative error of at most 0.0096.
Values may be sent and summed in bfloat16 or wider, within the bound.
No kernel may reach another device: no remote copies, remote signals or barrier semaphores. Data moves between devices by JAX's collectives and lax.ppermute only.
A program may use at most 128 MiB of HBM per device.

```python
import jax
import jax.numpy as jnp
from jax import lax

D = 768
HEAD_DIM = 64
HEADS = 6
VMAX = 128
BLK_DEV = 12
BLOCKS_XL = 192
HD = 384
N_IL = 16
N_XL = 16


def draw_vis_count(key, part):
    key_pair = jax.random.fold_in(key, 11)
    key_perm = jax.random.fold_in(key, 12)
    key_slot = jax.random.fold_in(key, 13)
    key_size = jax.random.fold_in(key, 14)
    half_xl = N_XL // 2
    lower = jax.random.randint(key_pair, (N_IL, half_xl), 0, BLK_DEV + 1)
    lower = lower.at[:, 0].set(BLK_DEV)
    loads = jnp.concatenate([lower, BLK_DEV - lower], axis=1)
    shuffle = jax.vmap(lambda k: jax.random.permutation(k, N_XL))(jax.random.split(key_perm, N_IL))
    loads = jnp.take_along_axis(loads, shuffle, axis=1)
    ranks = jax.vmap(lambda k: jax.random.permutation(k, BLK_DEV))(jax.random.split(key_slot, N_IL * N_XL))
    ranks = ranks.reshape(N_IL, N_XL, BLK_DEV)
    is_live = ranks < loads[:, :, None]
    sizes = jax.random.randint(key_size, (N_IL, N_XL, BLK_DEV), VMAX // 2, VMAX + 1)
    sizes = jnp.where(ranks == 0, VMAX, sizes)
    counts = jnp.where(is_live, sizes, 0)
    return counts.reshape(N_IL, N_XL * BLK_DEV).astype(jnp.int32)


def draw_patches(key, part):
    key_rows = jax.random.fold_in(key, 21)
    rows = jnp.clip(jax.random.normal(key_rows, (N_IL, BLOCKS_XL, VMAX, D), jnp.float32), -6.0, 6.0)
    return rows.astype(jnp.bfloat16)


def draw_w_qkv(key, part):
    key_base = jax.random.fold_in(key, 31)
    base = jnp.clip(jax.random.normal(key_base, (D, 3, HEADS, HEAD_DIM), jnp.float32), -6.0, 6.0)
    return (base * D ** (-0.5)).reshape(D, 3 * HEADS * HEAD_DIM).astype(jnp.bfloat16)


def block_scale(rng, shape, shards, low, largest):
    def one(dim, blocks):
        steps = jax.random.uniform(jax.random.fold_in(jax.random.fold_in(rng, 6), dim), (blocks,), jnp.float32, low / len(shards), largest / len(shards))
        return jnp.repeat(jnp.exp(steps), shape[dim] // blocks).reshape((-1,) + (1,) * (len(shape) - dim - 1))

    level = one(*shards[0])
    for cut in shards[1:]:
        level = level * one(*cut)
    return level


def gaussian(rng, dims, scale, most, cuts=(), kind=jnp.bfloat16):
    values = jax.random.normal(rng, dims, jnp.float32) * scale
    if len(cuts) > 0:
        values = block_scale(rng, dims, cuts, -0.22, 0.18) * values
    return jnp.clip(values, min=-most, max=most).astype(kind)


def setup_inputs(seed: int = 0) -> dict:
    key_list = jax.random.split(jax.random.key(seed), 7)
    patches = draw_patches(jax.random.fold_in(key_list[6], 71), 0)
    out_cot = gaussian(key_list[1], (N_IL, BLOCKS_XL, VMAX, D), 1.0, 6.0, ((0, 16), (1, 16)))
    vis_count = draw_vis_count(jax.random.fold_in(key_list[6], 71), 0)
    w_qkv = draw_w_qkv(jax.random.fold_in(key_list[6], 71), 0)
    w_out = gaussian(key_list[4], (D, HD), HD ** -0.5, 0.3125, ((0, 256),))
    ln_gain = jnp.clip(1.0 + 0.18 * jax.random.normal(key_list[5], (D,), jnp.float32), 0.1, 1.9)
    return {"patches": patches, "out_cot": out_cot, "vis_count": vis_count, "w_qkv": w_qkv, "w_out": w_out, "ln_gain": ln_gain}


def block_pass(tiles, cotan, counts, weights_qkv, weights_out, ln_gain):
    nblock, vrows, width = tiles.shape
    inner = HEADS * HEAD_DIM
    factor = HEAD_DIM ** (-0.5)
    positions = jnp.arange(vrows)
    row_mask = (positions[None, :] < counts[:, None]).astype(jnp.float32)
    tiles_f = tiles.astype(jnp.float32)
    centred = tiles_f - lax.optimization_barrier(jnp.mean(tiles_f, axis=-1, keepdims=True))
    inv_std = lax.rsqrt(lax.optimization_barrier(jnp.mean(centred * centred, axis=-1, keepdims=True)) + 1e-06)
    normed = centred * inv_std
    normed_b = (normed * ln_gain).astype(jnp.bfloat16).reshape(nblock * vrows, width)
    project = jnp.dot(normed_b, weights_qkv, preferred_element_type=jnp.float32).astype(jnp.bfloat16)
    project = project.reshape(nblock, vrows, 3, HEADS, HEAD_DIM)
    queries = project[:, :, 0].astype(jnp.float32)
    keys_f = project[:, :, 1].astype(jnp.float32)
    values_f = project[:, :, 2].astype(jnp.float32)
    scores = jnp.einsum('nqhe,nkhe->nhqk', queries, keys_f) * factor
    key_mask = (positions[None, :] < counts[:, None])[:, None, None, :]
    scores = jnp.where(key_mask, scores, jnp.float32(-1e+30))
    probs_f = jnp.exp(scores - lax.optimization_barrier(jnp.max(scores, axis=-1, keepdims=True)))
    probs_f = probs_f / lax.optimization_barrier(jnp.sum(probs_f, axis=-1, keepdims=True))
    probs_b = probs_f.astype(jnp.bfloat16).astype(jnp.float32)
    attended = jnp.einsum('nhqk,nkhe->nqhe', probs_b, values_f).astype(jnp.bfloat16).reshape(nblock * vrows, inner)
    mixed = jnp.dot(attended, weights_out.T, preferred_element_type=jnp.float32).reshape(nblock, vrows, width)
    encoded = ((tiles_f + mixed) * row_mask[..., None]).astype(jnp.bfloat16)
    grad_out = (cotan * row_mask[..., None].astype(jnp.bfloat16)).reshape(nblock * vrows, width)
    grad_wout = jnp.dot(grad_out.T, attended, preferred_element_type=jnp.float32)
    grad_att = jnp.dot(grad_out, weights_out, preferred_element_type=jnp.float32).astype(jnp.bfloat16)
    grad_att = grad_att.reshape(nblock, vrows, HEADS, HEAD_DIM).astype(jnp.float32)
    grad_prob = jnp.einsum('nqhe,nkhe->nhqk', grad_att, values_f)
    grad_val = jnp.einsum('nhqk,nqhe->nkhe', probs_b, grad_att)
    grad_score = probs_f * (grad_prob - lax.optimization_barrier(jnp.sum(probs_f * grad_prob, axis=-1, keepdims=True))) * factor
    grad_score = grad_score.astype(jnp.bfloat16).astype(jnp.float32)
    grad_query = jnp.einsum('nhqk,nkhe->nqhe', grad_score, keys_f)
    grad_key = jnp.einsum('nhqk,nqhe->nkhe', grad_score, queries)
    grad_proj = jnp.stack([grad_query, grad_key, grad_val], axis=2).astype(jnp.bfloat16).reshape(nblock * vrows, 3 * inner)
    grad_wqkv = jnp.dot(normed_b.T, grad_proj, preferred_element_type=jnp.float32)
    grad_norm = jnp.dot(grad_proj, weights_qkv.T, preferred_element_type=jnp.float32).reshape(nblock, vrows, width) * ln_gain
    grad_ln = inv_std * (grad_norm - lax.optimization_barrier(jnp.mean(grad_norm, axis=-1, keepdims=True)) - normed * lax.optimization_barrier(jnp.mean(grad_norm * normed, axis=-1, keepdims=True)))
    grad_rows = grad_out.reshape(nblock, vrows, width).astype(jnp.float32)
    grad_input = ((grad_rows + grad_ln) * row_mask[..., None]).astype(jnp.bfloat16)
    return (encoded, grad_input, grad_wqkv, grad_wout)

def reference(patches, out_cot, vis_count, w_qkv, w_out, ln_gain):

    def one_row(totals, row_items):
        tiles, cotan, counts = row_items
        encoded, grad_input, grad_qkv, grad_proj_out = block_pass(tiles, cotan, counts, w_qkv, w_out, ln_gain)
        return ((totals[0] + grad_qkv, totals[1] + grad_proj_out), (encoded, grad_input))
    start_totals = (jnp.zeros(w_qkv.shape, jnp.float32), jnp.zeros(w_out.shape, jnp.float32))
    totals, outputs = lax.scan(one_row, start_totals, (patches, out_cot, vis_count))
    return (outputs[0], outputs[1], totals[0], totals[1])
```

```python
import jax
import jax.numpy as jnp
from jax import lax
from jax.experimental import pallas as pl
from jax.experimental.pallas import tpu as pltpu
from jax.sharding import PartitionSpec as P

HEAD_DIM = 64
HEADS = 6
D = 768
HD = 384
VMAX = 128
GROUP = 2
ROWS = GROUP * VMAX
BF16 = jnp.bfloat16
F32 = jnp.float32


def hop_x(v, k):
    return lax.ppermute(v, "il", [(i, (i // 4) * 4 + (i + k) % 4) for i in range(16)])


def hop_y(v, k):
    return lax.ppermute(v, "il", [(i, (i + 4 * k) % 16) for i in range(16)])


def hop_z(v, k):
    return lax.ppermute(v, "xl", [(i, (i + 2 * k) % 16) for i in range(16)])


def hop_core(v):
    return lax.ppermute(v, "xl", [(i, i ^ 1) for i in range(16)])


def coords():
    il = lax.axis_index("il")
    xl = lax.axis_index("xl")
    return il // 4, il % 4, xl // 2, xl % 2


def gather4(v, hop, direct):
    r1 = hop(v, -1)
    r3 = hop(v, 1)
    if direct:
        r2 = hop(v, 2)
    else:
        h = v.shape[0] // 2
        r2 = jnp.concatenate([hop(r1[:h], -1), hop(r3[h:], 1)], axis=0)
    return [v, r1, r2, r3]


def gather_weights(w):
    y, x, z, c = coords()
    n = w.shape[1] // 2
    mine = lax.dynamic_slice(w, (0, c * n), (3, n))
    other = lax.dynamic_slice(w, (0, (1 - c) * n), (3, n))
    block = jnp.concatenate([mine, hop_core(other), jnp.zeros((2, n), w.dtype)], axis=0)
    stack = jnp.concatenate([block] + [hop_z(block, -k) for k in range(1, 8)], axis=0)
    r = jnp.arange(48)[:, None]
    s = jnp.arange(64)[None, :]
    j = s % 8
    row = ((z + s // 8) % 8) * 6 + (c ^ (j // 3)) * 3 + j % 3
    order = ((row == r) & (j < 6)).astype(w.dtype)
    v = jnp.dot(order, stack, preferred_element_type=F32).astype(w.dtype)
    v = jnp.concatenate(gather4(v, hop_x, True), axis=0)
    mine = gather4(v, hop_y, False)
    return mine + [hop_core(u) for u in mine]


def scatter4(parts, hop, direct, dt):
    if direct:
        got = [hop(parts[k].astype(dt), k) for k in (1, 2, 3)]
        return parts[0] + got[0].astype(F32) + got[1].astype(F32) + got[2].astype(F32)
    h = parts[2].shape[0] // 2
    far = parts[2].astype(dt)
    a = hop(far[:h], 1)
    b = hop(far[h:], -1)
    s1 = jnp.concatenate([parts[1][:h] + a.astype(F32), parts[1][h:]], axis=0).astype(dt)
    s3 = jnp.concatenate([parts[3][:h], parts[3][h:] + b.astype(F32)], axis=0).astype(dt)
    return parts[0] + hop(s1, 1).astype(F32) + hop(s3, -1).astype(F32)


def scatter_grads(keep, send):
    y, x, z, c = coords()
    n = keep.shape[1]
    total = keep + hop_core(send).astype(F32)
    rows = total.shape[0] // 4
    v = scatter4(
        [lax.dynamic_slice(total, (((y + k) % 4) * rows, 0), (rows, n)) for k in range(4)], hop_y, False, BF16
    )
    rows = rows // 4
    v = scatter4([lax.dynamic_slice(v, (((x + k) % 4) * rows, 0), (rows, n)) for k in range(4)], hop_x, True, F32)
    v = v.reshape(8, 6, n)
    v = lax.dynamic_slice(jnp.concatenate([v, v], axis=0), (z, 0, 0), (8, 6, n))
    acc = v[0]
    for k in range(1, 8):
        acc = acc + hop_z(v[k], k)
    mine = lax.dynamic_slice(acc, (3 * c, 0), (3, n))
    got = hop_core(lax.dynamic_slice(acc, (3 * (1 - c), 0), (3, n)))
    return jnp.concatenate([jnp.where(c == 0, mine, got), jnp.where(c == 0, got, mine)], axis=1)


def mm(a, b):
    return jnp.dot(a, b, preferred_element_type=F32)


def mm_t(a, b):
    return lax.dot_general(a, b, (((1,), (1,)), ((), ())), preferred_element_type=F32)


def tmm(a, b):
    return lax.dot_general(a, b, (((0,), (0,)), ((), ())), preferred_element_type=F32)


def layer_kernel(*refs):
    at_ref, counts_ref = refs[:2]
    pieces = refs[2:10]
    x_ref, cot_ref, gain_ref = refs[10:13]
    enc_ref, gin_ref, keep_ref, send_ref = refs[13:17]
    w_ref, nb_ref, go_ref, att_ref, gp_ref = refs[17:22]
    step = pl.program_id(0)
    factor = HEAD_DIM**-0.5
    core = at_ref[2]

    @pl.when(step == 0)
    def _():
        y, x = at_ref[0], at_ref[1]
        for rel in range(2):
            half = core ^ rel
            for ky in range(4):
                for kx in range(4):
                    row = ((y + ky) & 3) * 192 + ((x + kx) & 3) * 48
                    w_ref[half, pl.ds(pl.multiple_of(row, 16), 48), :] = pieces[rel * 4 + ky][kx * 48 : kx * 48 + 48, :]

    xf = x_ref[...].reshape(ROWS, D).astype(F32)
    gain = gain_ref[...]
    centred = xf - jnp.mean(xf, axis=-1, keepdims=True)
    inv = lax.rsqrt(jnp.mean(centred * centred, axis=-1, keepdims=True) + 1e-6)
    normed = centred * inv
    nb = (normed * gain).astype(BF16)
    row_id = lax.broadcasted_iota(jnp.int32, (VMAX, D), 0)
    masks = [row_id < counts_ref[step * GROUP + b] for b in range(GROUP)]
    mask = jnp.concatenate(masks, axis=0)
    cot = cot_ref[...].reshape(ROWS, D)
    go_f = jnp.where(mask, cot.astype(F32), 0.0)
    go = go_f.astype(BF16)
    at = pl.ds(pl.multiple_of(step * ROWS, ROWS), ROWS)
    nb_ref[at, :] = nb
    go_ref[at, :] = go

    w0 = w_ref[0]
    wv = w_ref[1, :, :HD]
    wo = w_ref[1, :, HD:]
    qk = mm(nb, w0).astype(BF16)
    vv = mm(nb, wv).astype(BF16)
    ga = mm(go, wo).astype(BF16)
    key_id = lax.broadcasted_iota(jnp.int32, (VMAX, VMAX), 1)
    for b in range(GROUP):
        live = key_id < counts_ref[step * GROUP + b]
        rs = slice(b * VMAX, (b + 1) * VMAX)
        atts, gqs, gks, gvs = [], [], [], []
        for h in range(HEADS):
            lo = h * HEAD_DIM
            q = qk[rs, lo : lo + HEAD_DIM]
            k = qk[rs, HD + lo : HD + lo + HEAD_DIM]
            v = vv[rs, lo : lo + HEAD_DIM]
            g = ga[rs, lo : lo + HEAD_DIM]
            s = jnp.where(live, mm_t(q, k) * factor, -1e30)
            e = jnp.exp(s - jnp.max(s, axis=-1, keepdims=True))
            p = e / jnp.sum(e, axis=-1, keepdims=True)
            pb = p.astype(BF16)
            atts.append(mm(pb, v).astype(BF16))
            dp = mm_t(g, v)
            gvs.append(tmm(pb, g).astype(BF16))
            ds = (p * (dp - jnp.sum(p * dp, axis=-1, keepdims=True)) * factor).astype(BF16)
            gqs.append(mm(ds, k).astype(BF16))
            gks.append(tmm(ds, q).astype(BF16))
        at_b = pl.ds(pl.multiple_of(step * ROWS + b * VMAX, VMAX), VMAX)
        att_ref[at_b, :] = jnp.concatenate(atts, axis=1)
        gp_ref[at_b, :] = jnp.concatenate(gqs + gks + gvs, axis=1)

    mixed = mm_t(att_ref[at, :], wo)
    enc_ref[...] = jnp.where(mask, xf + mixed, 0.0).astype(BF16).reshape(GROUP, VMAX, D)
    gp = gp_ref[at, :]
    gn = (mm_t(gp[:, :D], w0) + mm_t(gp[:, D:], wv)) * gain
    gl = inv * (
        gn - jnp.mean(gn, axis=-1, keepdims=True) - normed * jnp.mean(gn * normed, axis=-1, keepdims=True)
    )
    gin_ref[...] = jnp.where(mask, go_f + gl, 0.0).astype(BF16).reshape(GROUP, VMAX, D)

    @pl.when(step == pl.num_programs(0) - 1)
    def _():
        for r in range(0, D, 256):
            rr = slice(r, r + 256)
            nbt = nb_ref[:, rr]
            got = go_ref[:, rr]
            for half, cols, val in (
                (0, slice(0, D), tmm(nbt, gp_ref[:, :D])),
                (1, slice(0, HD), tmm(nbt, gp_ref[:, D:])),
                (1, slice(HD, D), tmm(got, att_ref[...])),
            ):

                @pl.when(core == half)
                def _():
                    keep_ref[rr, cols] = val

                @pl.when(core != half)
                def _():
                    send_ref[rr, cols] = val.astype(send_ref.dtype)


def layer(at, counts, pieces, tiles, cotan, gain):
    nblock = tiles.shape[0]
    whole = lambda shape: pl.BlockSpec(shape, lambda i, *_: (0,) * len(shape), pipeline_mode=pl.Buffered(1))
    tile = pl.BlockSpec((GROUP, VMAX, D), lambda i, *_: (i, 0, 0))
    rows = nblock * VMAX
    return pl.pallas_call(
        layer_kernel,
        grid_spec=pltpu.PrefetchScalarGridSpec(
            num_scalar_prefetch=2,
            grid=(nblock // GROUP,),
            in_specs=[whole((192, D))] * 8 + [tile, tile, whole((1, D))],
            out_specs=[tile, tile, whole((D, D)), whole((D, D))],
            scratch_shapes=[
                pltpu.VMEM((2, D, D), BF16),
                pltpu.VMEM((rows, D), BF16),
                pltpu.VMEM((rows, D), BF16),
                pltpu.VMEM((rows, HD), BF16),
                pltpu.VMEM((rows, 3 * HD), BF16),
            ],
        ),
        out_shape=[
            jax.ShapeDtypeStruct(tiles.shape, BF16),
            jax.ShapeDtypeStruct(tiles.shape, BF16),
            jax.ShapeDtypeStruct((D, D), F32),
            jax.ShapeDtypeStruct((D, D), F32),
        ],
        compiler_params=pltpu.CompilerParams(
            dimension_semantics=("arbitrary",), vmem_limit_bytes=48 * 1024 * 1024
        ),
        cost_estimate=pl.CostEstimate(flops=14_000_000_000, bytes_accessed=20_000_000, transcendentals=1_200_000),
    )(at, counts, *pieces, tiles, cotan, gain)


def shards(patches, out_cot, vis_count, w_qkv, w_out, ln_gain):
    y, x, z, c = coords()
    pieces = gather_weights(jnp.concatenate([w_qkv, w_out], axis=1))
    at = jnp.stack([y, x, c]).astype(jnp.int32)
    enc, gin, keep, send = layer(at, vis_count[0], pieces, patches[0], out_cot[0], ln_gain[None])
    grads = scatter_grads(keep, send)
    n = w_qkv.shape[1]
    return enc[None], gin[None], grads[:, :n], grads[:, n:]


def solution(mesh):
    return jax.shard_map(
        shards,
        mesh=mesh,
        in_specs=(
            P("il", "xl", None, None),
            P("il", "xl", None, None),
            P("il", "xl"),
            P(("il", "xl"), None),
            P(("il", "xl"), None),
            P(),
        ),
        out_specs=(
            P("il", "xl", None, None),
            P("il", "xl", None, None),
            P(("il", "xl"), None),
            P(("il", "xl"), None),
        ),
        check_vma=False,
    )
```

```python
import jax
import jax.numpy as jnp
from jax import lax
from jax.experimental import pallas as pl
from jax.experimental.pallas import tpu as pltpu
from jax.sharding import PartitionSpec as P

HEAD_DIM = 64
HEADS = 6
D = 768
HD = 384
VMAX = 128
GROUP = 4
ROWS = GROUP * VMAX
BF16 = jnp.bfloat16
F32 = jnp.float32


def hop_x(v, k):
    return lax.ppermute(v, "il", [(i, (i // 4) * 4 + (i + k) % 4) for i in range(16)])


def hop_y(v, k):
    return lax.ppermute(v, "il", [(i, (i + 4 * k) % 16) for i in range(16)])


def hop_z(v, k):
    return lax.ppermute(v, "xl", [(i, (i + 2 * k) % 16) for i in range(16)])


def hop_core(v):
    return lax.ppermute(v, "xl", [(i, i ^ 1) for i in range(16)])


def coords():
    il = lax.axis_index("il")
    xl = lax.axis_index("xl")
    return il // 4, il % 4, xl // 2, xl % 2


def gather4(v, hop, direct):
    r1 = hop(v, -1)
    r3 = hop(v, 1)
    if direct:
        r2 = hop(v, 2)
    else:
        h = v.shape[0] // 2
        r2 = jnp.concatenate([hop(r1[:h], -1), hop(r3[h:], 1)], axis=0)
    return [v, r1, r2, r3]


def gather_weights(w):
    y, x, z, c = coords()
    n = w.shape[1] // 2
    mine = lax.dynamic_slice(w, (0, c * n), (3, n))
    other = lax.dynamic_slice(w, (0, (1 - c) * n), (3, n))
    block = jnp.concatenate([mine, hop_core(other), jnp.zeros((2, n), w.dtype)], axis=0)
    block = jnp.concatenate([block, lax.ppermute(block, "xl", [(i, i ^ 2) for i in range(16)])], axis=0)
    stack = jnp.concatenate([block, hop_z(block, 2), hop_z(block, -2), hop_z(block, 4)], axis=0)
    r = jnp.arange(48)[:, None]
    s = jnp.arange(64)[None, :]
    slot = s // 16
    j = s % 8
    origin = (z + jnp.where(slot == 3, 4, jnp.where(slot == 2, 2, jnp.where(slot == 1, 6, 0)))) % 8
    row = (origin ^ ((s // 8) % 2)) * 6 + (c ^ (j // 3)) * 3 + j % 3
    order = ((row == r) & (j < 6)).astype(w.dtype)
    v = jnp.dot(order, stack, preferred_element_type=F32).astype(w.dtype)
    v = jnp.concatenate(gather4(v, hop_x, True), axis=0)
    mine = gather4(v, hop_y, True)
    return mine + [hop_core(u) for u in mine]


def scatter4(parts, hop, direct, dt):
    if direct:
        got = [hop(parts[k].astype(dt), k) for k in (1, 2, 3)]
        return parts[0] + got[0].astype(F32) + got[1].astype(F32) + got[2].astype(F32)
    h = parts[2].shape[0] // 2
    far = parts[2].astype(dt)
    a = hop(far[:h], 1)
    b = hop(far[h:], -1)
    s1 = jnp.concatenate([parts[1][:h] + a.astype(F32), parts[1][h:]], axis=0).astype(dt)
    s3 = jnp.concatenate([parts[3][:h], parts[3][h:] + b.astype(F32)], axis=0).astype(dt)
    return parts[0] + hop(s1, 1).astype(F32) + hop(s3, -1).astype(F32)


def scatter_grads(keep, send):
    y, x, z, c = coords()
    n = keep.shape[1]
    total = keep + hop_core(send).astype(F32)
    rows = total.shape[0] // 4
    v = scatter4(
        [lax.dynamic_slice(total, (((y + k) % 4) * rows, 0), (rows, n)) for k in range(4)], hop_y, False, BF16
    )
    rows = rows // 4
    v = scatter4([lax.dynamic_slice(v, (((x + k) % 4) * rows, 0), (rows, n)) for k in range(4)], hop_x, True, F32)
    got = lax.all_to_all(v.reshape(16, 3, n), "xl", split_axis=0, concat_axis=0, tiled=True)
    acc = jnp.sum(got.reshape(8, 2, 3, n), axis=0)
    return jnp.concatenate([acc[0], acc[1]], axis=1)


def mm(a, b):
    return jnp.dot(a, b, preferred_element_type=F32)


def mm_t(a, b):
    return lax.dot_general(a, b, (((1,), (1,)), ((), ())), preferred_element_type=F32)


def tmm(a, b):
    return lax.dot_general(a, b, (((0,), (0,)), ((), ())), preferred_element_type=F32)


def layer_kernel(*refs):
    at_ref, counts_ref = refs[:2]
    pieces = refs[2:10]
    x_ref, cot_ref, gain_ref = refs[10:13]
    enc_ref, gin_ref, keep_ref, send_ref = refs[13:17]
    w_ref, nb_ref, go_ref, att_ref, gp_ref, sems = refs[17:23]
    step = pl.program_id(0)
    factor = HEAD_DIM**-0.5
    core = at_ref[2]

    @pl.when(step == 0)
    def _():
        y, x = at_ref[0], at_ref[1]
        copies = []
        for rel in range(2):
            half = core ^ rel
            for ky in range(4):
                for kx in range(4):
                    row = pl.multiple_of(((y + ky) & 3) * 192 + ((x + kx) & 3) * 48, 16)
                    copies.append(
                        pltpu.make_async_copy(
                            pieces[rel * 4 + ky].at[pl.ds(kx * 48, 48), :],
                            w_ref.at[half, pl.ds(row, 48), :],
                            sems.at[len(copies)],
                        )
                    )
        for copy in copies:
            copy.start()
        for copy in copies:
            copy.wait()

    xf = x_ref[...].reshape(ROWS, D).astype(F32)
    gain = gain_ref[...]
    centred = xf - jnp.mean(xf, axis=-1, keepdims=True)
    inv = lax.rsqrt(jnp.mean(centred * centred, axis=-1, keepdims=True) + 1e-6)
    normed = centred * inv
    nb = (normed * gain).astype(BF16)
    row_id = lax.broadcasted_iota(jnp.int32, (VMAX, D), 0)
    masks = [row_id < counts_ref[step * GROUP + b] for b in range(GROUP)]
    mask = jnp.concatenate(masks, axis=0)
    cot = cot_ref[...].reshape(ROWS, D)
    go_f = jnp.where(mask, cot.astype(F32), 0.0)
    go = go_f.astype(BF16)
    at = pl.ds(pl.multiple_of(step * ROWS, ROWS), ROWS)
    nb_ref[at, :] = nb
    go_ref[at, :] = go

    w0 = w_ref[0]
    wv = w_ref[1, :, :HD]
    wo = w_ref[1, :, HD:]
    qk = mm(nb, w0).astype(BF16)
    vv = mm(nb, wv).astype(BF16)
    ga = mm(go, wo).astype(BF16)
    key_id = lax.broadcasted_iota(jnp.int32, (VMAX, 2 * VMAX), 0)
    lane = lax.broadcasted_iota(jnp.int32, (1, 2 * HEAD_DIM), 1)
    first = jnp.where(lane < HEAD_DIM, 1.0, 0.0)
    m0, m1 = first.astype(BF16), (1.0 - first).astype(BF16)
    f0, f1 = (first * factor).astype(BF16), ((1.0 - first) * factor).astype(BF16)
    pair = lambda a, u, w: jnp.concatenate([a * u, a * w], axis=0)
    for b in range(GROUP):
        live = key_id < counts_ref[step * GROUP + b]
        rs = slice(b * VMAX, (b + 1) * VMAX)
        at_b = pl.ds(pl.multiple_of(step * ROWS + b * VMAX, VMAX), VMAX)
        for lo in range(0, HD, 2 * HEAD_DIM):
            hi = lo + 2 * HEAD_DIM
            k = qk[rs, HD + lo : HD + hi]
            v = vv[rs, lo:hi]
            q2 = pair(qk[rs, lo:hi], f0, f1)
            g2 = pair(ga[rs, lo:hi], m0, m1)
            s = jnp.where(live, mm_t(k, q2), -1e30)
            e = jnp.exp(s - jnp.max(s, axis=0, keepdims=True))
            p = e * (1.0 / jnp.sum(e, axis=0, keepdims=True))
            pb = p.astype(BF16)
            dp = mm_t(v, g2)
            ds = (p * (dp - jnp.sum(p * dp, axis=0, keepdims=True))).astype(BF16)
            stack = lambda a: jnp.concatenate([a[:, :VMAX], a[:, VMAX:]], axis=0)
            att_ref[at_b, lo:hi] = tmm(stack(pb), pair(v, m0, m1)).astype(BF16)
            gp_ref[at_b, lo:hi] = tmm(stack(ds), pair(k, f0, f1)).astype(BF16)
            gp_ref[at_b, HD + lo : HD + hi] = mm(ds, q2).astype(BF16)
            gp_ref[at_b, D + lo : D + hi] = mm(pb, g2).astype(BF16)

    mixed = mm_t(att_ref[at, :], wo)
    enc_ref[...] = jnp.where(mask, xf + mixed, 0.0).astype(BF16).reshape(GROUP, VMAX, D)
    gp = gp_ref[at, :]
    gn = (mm_t(gp[:, :D], w0) + mm_t(gp[:, D:], wv)) * gain
    gl = inv * (
        gn - jnp.mean(gn, axis=-1, keepdims=True) - normed * jnp.mean(gn * normed, axis=-1, keepdims=True)
    )
    gin_ref[...] = jnp.where(mask, go_f + gl, 0.0).astype(BF16).reshape(GROUP, VMAX, D)

    @pl.when(step == pl.num_programs(0) - 1)
    def _():
        for r in range(0, D, 256):
            rr = slice(r, r + 256)
            gw = tmm(nb_ref[:, rr], gp_ref[...])
            got = go_ref[:, rr]
            for half, cols, val in (
                (0, slice(0, D), gw[:, :D]),
                (1, slice(0, HD), gw[:, D:]),
                (1, slice(HD, D), tmm(got, att_ref[...])),
            ):

                @pl.when(core == half)
                def _():
                    keep_ref[rr, cols] = val

                @pl.when(core != half)
                def _():
                    send_ref[rr, cols] = val.astype(send_ref.dtype)


def layer(at, counts, pieces, tiles, cotan, gain):
    nblock = tiles.shape[0]
    whole = lambda shape: pl.BlockSpec(shape, lambda i, *_: (0,) * len(shape), pipeline_mode=pl.Buffered(1))
    tile = pl.BlockSpec((GROUP, VMAX, D), lambda i, *_: (i, 0, 0))
    rows = nblock * VMAX
    return pl.pallas_call(
        layer_kernel,
        grid_spec=pltpu.PrefetchScalarGridSpec(
            num_scalar_prefetch=2,
            grid=(nblock // GROUP,),
            in_specs=[pl.BlockSpec(memory_space=pl.ANY)] * 8 + [tile, tile, whole((1, D))],
            out_specs=[tile, tile, whole((D, D)), whole((D, D))],
            scratch_shapes=[
                pltpu.VMEM((2, D, D), BF16),
                pltpu.VMEM((rows, D), BF16),
                pltpu.VMEM((rows, D), BF16),
                pltpu.VMEM((rows, HD), BF16),
                pltpu.VMEM((rows, 3 * HD), BF16),
                pltpu.SemaphoreType.DMA((32,)),
            ],
        ),
        out_shape=[
            jax.ShapeDtypeStruct(tiles.shape, BF16),
            jax.ShapeDtypeStruct(tiles.shape, BF16),
            jax.ShapeDtypeStruct((D, D), F32),
            jax.ShapeDtypeStruct((D, D), F32),
        ],
        compiler_params=pltpu.CompilerParams(
            dimension_semantics=("arbitrary",), vmem_limit_bytes=48 * 1024 * 1024
        ),
        cost_estimate=pl.CostEstimate(flops=14_000_000_000, bytes_accessed=20_000_000, transcendentals=1_200_000),
    )(at, counts, *pieces, tiles, cotan, gain)


def shards(patches, out_cot, vis_count, w_qkv, w_out, ln_gain):
    y, x, z, c = coords()
    pieces = gather_weights(jnp.concatenate([w_qkv, w_out], axis=1))
    at = jnp.stack([y, x, c]).astype(jnp.int32)
    enc, gin, keep, send = layer(at, vis_count[0], pieces, patches[0], out_cot[0], ln_gain[None])
    grads = scatter_grads(keep, send)
    n = w_qkv.shape[1]
    return enc[None], gin[None], grads[:, :n], grads[:, n:]


def solution(mesh):
    return jax.shard_map(
        shards,
        mesh=mesh,
        in_specs=(
            P("il", "xl", None, None),
            P("il", "xl", None, None),
            P("il", "xl"),
            P(("il", "xl"), None),
            P(("il", "xl"), None),
            P(),
        ),
        out_specs=(
            P("il", "xl", None, None),
            P("il", "xl", None, None),
            P(("il", "xl"), None),
            P(("il", "xl"), None),
        ),
        check_vma=False,
    )
```

```python
import functools

import jax
import jax.numpy as jnp
from jax import lax
from jax.experimental import pallas as pl
from jax.experimental.pallas import tpu as pltpu
from jax.sharding import PartitionSpec as P

HEAD_DIM = 64
HEADS = 6
D = 768
HD = 384
VMAX = 128
BLOCKS = 12
GROUP = 4
ROWS = GROUP * VMAX
BF16 = jnp.bfloat16
F32 = jnp.float32


def hop_x(v, k):
    return lax.ppermute(v, "il", [(i, (i // 4) * 4 + (i + k) % 4) for i in range(16)])


def hop_y(v, k):
    return lax.ppermute(v, "il", [(i, (i + 4 * k) % 16) for i in range(16)])


def hop_z(v, k):
    return lax.ppermute(v, "xl", [(i, (i + 2 * k) % 16) for i in range(16)])


def hop_core(v):
    return lax.ppermute(v, "xl", [(i, i ^ 1) for i in range(16)])


def coords():
    il = lax.axis_index("il")
    xl = lax.axis_index("xl")
    return il // 4, il % 4, xl // 2, xl % 2


def gather4(v, hop, direct):
    r1 = hop(v, -1)
    r3 = hop(v, 1)
    if direct:
        r2 = hop(v, 2)
    else:
        h = v.shape[0] // 2
        r2 = jnp.concatenate([hop(r1[:h], -1), hop(r3[h:], 1)], axis=0)
    return [v, r1, r2, r3]


def gather_weights(w):
    y, x, z, c = coords()
    n = w.shape[1] // 2
    mine = lax.dynamic_slice(w, (0, c * n), (3, n))
    other = lax.dynamic_slice(w, (0, (1 - c) * n), (3, n))
    block = jnp.concatenate([mine, hop_core(other), jnp.zeros((2, n), w.dtype)], axis=0)
    block = jnp.concatenate([block, lax.ppermute(block, "xl", [(i, i ^ 2) for i in range(16)])], axis=0)
    stack = jnp.concatenate([block, hop_z(block, 2), hop_z(block, -2), hop_z(block, 4)], axis=0)
    r = jnp.arange(48)[:, None]
    s = jnp.arange(64)[None, :]
    slot = s // 16
    j = s % 8
    origin = (z + jnp.where(slot == 3, 4, jnp.where(slot == 2, 2, jnp.where(slot == 1, 6, 0)))) % 8
    row = (origin ^ ((s // 8) % 2)) * 6 + (c ^ (j // 3)) * 3 + j % 3
    order = ((row == r) & (j < 6)).astype(w.dtype)
    v = jnp.dot(order, stack, preferred_element_type=F32).astype(w.dtype)
    v = jnp.concatenate(gather4(v, hop_x, True), axis=0)
    mine = gather4(v, hop_y, True)
    return mine + [hop_core(u) for u in mine]


def scatter4(parts, hop):
    got = [hop(parts[k].astype(BF16), k) for k in (1, 2, 3)]
    return parts[0] + got[0].astype(F32) + got[1].astype(F32) + got[2].astype(F32)


def scatter_grads(at, keep, send):
    y, x, z, c = coords()
    n = keep.shape[1]
    v = scatter4(split_rows(at, keep, hop_core(send)), hop_y)
    rows = v.shape[0] // 4
    v = scatter4([lax.dynamic_slice(v, (((x + k) % 4) * rows, 0), (rows, n)) for k in range(4)], hop_x)
    got = lax.all_to_all(v.reshape(16, 3, n), "xl", split_axis=0, concat_axis=0, tiled=True)
    acc = jnp.sum(got.reshape(8, 2, 3, n), axis=0)
    return jnp.concatenate([acc[0], acc[1]], axis=1)


def mm(a, b):
    return jnp.dot(a, b, preferred_element_type=F32)


def mm_t(a, b):
    return lax.dot_general(a, b, (((1,), (1,)), ((), ())), preferred_element_type=F32)


def tmm(a, b):
    return lax.dot_general(a, b, (((0,), (0,)), ((), ())), preferred_element_type=F32)


def norm_rows(xf):
    centred = xf - jnp.mean(xf, axis=-1, keepdims=True)
    inv = lax.rsqrt(jnp.mean(centred * centred, axis=-1, keepdims=True) + 1e-6)
    return centred * inv, inv


def row_mask(counts_ref, first, group):
    row_id = lax.broadcasted_iota(jnp.int32, (VMAX, D), 0)
    return jnp.concatenate([row_id < counts_ref[first + b] for b in range(group)], axis=0)


def core_kernel(*refs):
    at_ref, counts_ref = refs[:2]
    pieces = refs[2:10]
    x_ref, cot_ref, gain_ref = refs[10:13]
    w_out, att_out, gp_out, keep_out, send_out = refs[13:18]
    w_ref, nb_ref, go_ref, att_ref, gp_ref, keep_ref, send_ref, w_sems, row_sems, dw_sems = refs[18:]
    step = pl.program_id(0)
    last = pl.num_programs(0) - 1
    factor = HEAD_DIM**-0.5
    core = at_ref[2]

    @pl.when(step == 0)
    def _():
        y, x = at_ref[0], at_ref[1]
        copies = []
        for rel in range(2):
            half = core ^ rel
            for ky in range(4):
                for kx in range(4):
                    row = pl.multiple_of(((y + ky) & 3) * 192 + ((x + kx) & 3) * 48, 16)
                    copies.append(
                        pltpu.make_async_copy(
                            pieces[rel * 4 + ky].at[pl.ds(kx * 48, 48), :],
                            w_ref.at[half, pl.ds(row, 48), :],
                            w_sems.at[len(copies)],
                        )
                    )
        for copy in copies:
            copy.start()
        for copy in copies:
            copy.wait()

    whole_w = pltpu.make_async_copy(w_ref, w_out, w_sems.at[32])

    @pl.when(step == 0)
    def _():
        whole_w.start()

    normed, _ = norm_rows(x_ref[...].reshape(ROWS, D).astype(F32))
    nb = (normed * gain_ref[...]).astype(BF16)
    mask = row_mask(counts_ref, step * GROUP, GROUP)
    go = jnp.where(mask, cot_ref[...].reshape(ROWS, D).astype(F32), 0.0).astype(BF16)
    at = pl.ds(pl.multiple_of(step * ROWS, ROWS), ROWS)
    nb_ref[at, :] = nb
    go_ref[at, :] = go

    qk = mm(nb, w_ref[0]).astype(BF16)
    vv = mm(nb, w_ref[1, :, :HD]).astype(BF16)
    ga = mm(go, w_ref[1, :, HD:]).astype(BF16)
    key_id = lax.broadcasted_iota(jnp.int32, (VMAX, 2 * VMAX), 0)
    lane = lax.broadcasted_iota(jnp.int32, (1, 2 * HEAD_DIM), 1)
    first = jnp.where(lane < HEAD_DIM, 1.0, 0.0)
    m0, m1 = first.astype(BF16), (1.0 - first).astype(BF16)
    f0, f1 = (first * factor).astype(BF16), ((1.0 - first) * factor).astype(BF16)
    pair = lambda a, u, w: jnp.concatenate([a * u, a * w], axis=0)
    stack = lambda a: jnp.concatenate([a[:, :VMAX], a[:, VMAX:]], axis=0)
    for b in range(GROUP):
        live = key_id < counts_ref[step * GROUP + b]
        rs = slice(b * VMAX, (b + 1) * VMAX)
        at_b = pl.ds(pl.multiple_of(step * ROWS + b * VMAX, VMAX), VMAX)
        for lo in range(0, HD, 2 * HEAD_DIM):
            hi = lo + 2 * HEAD_DIM
            k = qk[rs, HD + lo : HD + hi]
            v = vv[rs, lo:hi]
            q2 = pair(qk[rs, lo:hi], f0, f1)
            g2 = pair(ga[rs, lo:hi], m0, m1)
            s = jnp.where(live, mm_t(k, q2), -1e30)
            e = jnp.exp(s - jnp.max(s, axis=0, keepdims=True))
            p = e * (1.0 / jnp.sum(e, axis=0, keepdims=True))
            pb = p.astype(BF16)
            dp = mm_t(v, g2)
            ds = (p * (dp - jnp.sum(p * dp, axis=0, keepdims=True))).astype(BF16)
            att_ref[at_b, lo:hi] = tmm(stack(pb), pair(v, m0, m1)).astype(BF16)
            gp_ref[at_b, lo:hi] = tmm(stack(ds), pair(k, f0, f1)).astype(BF16)
            gp_ref[at_b, HD + lo : HD + hi] = mm(ds, q2).astype(BF16)
            gp_ref[at_b, D + lo : D + hi] = mm(pb, g2).astype(BF16)

    def row_copies(i):
        rows = pl.ds(pl.multiple_of(i * ROWS, ROWS), ROWS)
        return (
            pltpu.make_async_copy(att_ref.at[rows, :], att_out.at[rows, :], row_sems.at[0, i]),
            pltpu.make_async_copy(gp_ref.at[rows, :], gp_out.at[rows, :], row_sems.at[1, i]),
        )

    for copy in row_copies(step):
        copy.start()

    @pl.when(step == last)
    def _():
        copies = []
        for i in range(D // 256):
            rr = slice(i * 256, i * 256 + 256)
            gw = tmm(nb_ref[:, rr], gp_ref[...])
            for half, cols, val in (
                (0, slice(0, D), gw[:, :D]),
                (1, slice(0, HD), gw[:, D:]),
                (1, slice(HD, D), tmm(go_ref[:, rr], att_ref[...])),
            ):

                @pl.when(core == half)
                def _():
                    keep_ref[rr, cols] = val

                @pl.when(core != half)
                def _():
                    send_ref[rr, cols] = val.astype(send_ref.dtype)

            copies.append(pltpu.make_async_copy(keep_ref.at[rr, :], keep_out.at[rr, :], dw_sems.at[0, i]))
            copies.append(pltpu.make_async_copy(send_ref.at[rr, :], send_out.at[rr, :], dw_sems.at[1, i]))
            copies[-1].start()
            copies[-2].start()
        whole_w.wait()
        for i in range(BLOCKS // GROUP):
            for copy in row_copies(i):
                copy.wait()
        for copy in copies:
            copy.wait()


def grads_core(at, counts, pieces, tiles, cotan, gain):
    nblock = tiles.shape[0]
    rows = nblock * VMAX
    hbm = pl.BlockSpec(memory_space=pltpu.HBM)
    tile = pl.BlockSpec((GROUP, VMAX, D), lambda i, *_: (i, 0, 0))
    return pl.pallas_call(
        core_kernel,
        grid_spec=pltpu.PrefetchScalarGridSpec(
            num_scalar_prefetch=2,
            grid=(nblock // GROUP,),
            in_specs=[hbm] * 8 + [tile, tile, pl.BlockSpec((1, D), lambda i, *_: (0, 0))],
            out_specs=[hbm] * 5,
            scratch_shapes=[
                pltpu.VMEM((2, D, D), BF16),
                pltpu.VMEM((rows, D), BF16),
                pltpu.VMEM((rows, D), BF16),
                pltpu.VMEM((rows, HD), BF16),
                pltpu.VMEM((rows, 3 * HD), BF16),
                pltpu.VMEM((D, D), F32),
                pltpu.VMEM((D, D), BF16),
                pltpu.SemaphoreType.DMA((33,)),
                pltpu.SemaphoreType.DMA((2, nblock // GROUP)),
                pltpu.SemaphoreType.DMA((2, D // 256)),
            ],
        ),
        out_shape=[
            jax.ShapeDtypeStruct((2, D, D), BF16),
            jax.ShapeDtypeStruct((rows, HD), BF16),
            jax.ShapeDtypeStruct((rows, 3 * HD), BF16),
            jax.ShapeDtypeStruct((D, D), F32),
            jax.ShapeDtypeStruct((D, D), BF16),
        ],
        compiler_params=pltpu.CompilerParams(
            dimension_semantics=("arbitrary",), vmem_limit_bytes=56 * 1024 * 1024
        ),
        cost_estimate=pl.CostEstimate(flops=20_000_000_000, bytes_accessed=18_000_000, transcendentals=1_200_000),
    )(at, counts, *pieces, tiles, cotan, gain)


def rows_kernel(first, counts_ref, w_ref, att_ref, gp_ref, x_ref, cot_ref, gain_ref, *rest):
    enc_ref, gin_ref = rest[-2:]
    gain = gain_ref[...]
    xf = x_ref[...].reshape(ROWS, D).astype(F32)
    normed, inv = norm_rows(xf)
    mask = row_mask(counts_ref, (first + pl.program_id(0)) * GROUP, GROUP)
    enc = xf + mm_t(att_ref[...], w_ref[1, :, HD:])
    enc_ref[...] = jnp.where(mask, enc, 0.0).astype(BF16).reshape(GROUP, VMAX, D)
    gp = gp_ref[...]
    gn = (mm_t(gp[:, :D], w_ref[0]) + mm_t(gp[:, D:], w_ref[1, :, :HD])) * gain
    gl = inv * (
        gn - jnp.mean(gn, axis=-1, keepdims=True) - normed * jnp.mean(gn * normed, axis=-1, keepdims=True)
    )
    gin = cot_ref[...].reshape(ROWS, D).astype(F32) + gl
    gin_ref[...] = jnp.where(mask, gin, 0.0).astype(BF16).reshape(GROUP, VMAX, D)


def rows_part(first, count, counts, w, att, gp, tiles, cotan, gain, done):
    tile = pl.BlockSpec((GROUP, VMAX, D), lambda i, *_: (i + first, 0, 0))
    flat = lambda cols: pl.BlockSpec((ROWS, cols), lambda i, *_: (i + first, 0))
    return pl.pallas_call(
        functools.partial(rows_kernel, first),
        grid_spec=pltpu.PrefetchScalarGridSpec(
            num_scalar_prefetch=1,
            grid=(count,),
            in_specs=[
                pl.BlockSpec((2, D, D), lambda i, *_: (0, 0, 0), pipeline_mode=pl.Buffered(1)),
                flat(HD),
                flat(3 * HD),
                tile,
                tile,
                pl.BlockSpec((1, D), lambda i, *_: (0, 0)),
            ]
            + [pl.BlockSpec(memory_space=pltpu.HBM)] * len(done),
            out_specs=[tile, tile],
        ),
        out_shape=[jax.ShapeDtypeStruct(tiles.shape, BF16)] * 2,
        input_output_aliases={7 + i: i for i in range(len(done))},
        compiler_params=pltpu.CompilerParams(
            dimension_semantics=("arbitrary",), vmem_limit_bytes=40 * 1024 * 1024
        ),
        cost_estimate=pl.CostEstimate(
            flops=count * 1_300_000_000, bytes_accessed=count * 5_000_000, transcendentals=1000
        ),
    )(counts, w, att, gp, tiles, cotan, gain, *done)


def split_kernel(at_ref, keep_ref, got_ref, own_ref, *outs):
    step = pl.program_id(0)
    total = keep_ref[...] + got_ref[...].astype(F32)

    @pl.when(step == 0)
    def _():
        own_ref[...] = total

    for k in range(1, 4):

        @pl.when(step == k)
        def _():
            outs[k - 1][...] = total.astype(BF16)


def split_rows(at, keep, got):
    rows = keep.shape[0] // 4
    n = keep.shape[1]
    block = pl.BlockSpec((rows, n), lambda i, at: ((at[0] + i) % 4, 0))
    out = pl.BlockSpec((rows, n), lambda i, at: (0, 0))
    return pl.pallas_call(
        split_kernel,
        grid_spec=pltpu.PrefetchScalarGridSpec(
            num_scalar_prefetch=1, grid=(4,), in_specs=[block, block], out_specs=[out] * 4
        ),
        out_shape=[jax.ShapeDtypeStruct((rows, n), F32)] + [jax.ShapeDtypeStruct((rows, n), BF16)] * 3,
        compiler_params=pltpu.CompilerParams(dimension_semantics=("arbitrary",)),
        cost_estimate=pl.CostEstimate(flops=600_000, bytes_accessed=5_000_000, transcendentals=0),
    )(at, keep, got)


def shards(patches, out_cot, vis_count, w_qkv, w_out, ln_gain):
    y, x, z, c = coords()
    pieces = gather_weights(jnp.concatenate([w_qkv, w_out], axis=1))
    at = jnp.stack([y, x, c]).astype(jnp.int32)
    counts, tiles, cotan, gain = vis_count[0], patches[0], out_cot[0], ln_gain[None]
    w, att, gp, keep, send = grads_core(at, counts, pieces, tiles, cotan, gain)
    out = rows_part(0, 1, counts, w, att, gp, tiles, cotan, gain, ())
    enc, gin = rows_part(1, 2, counts, w, att, gp, tiles, cotan, gain, out)
    grads = scatter_grads(at, keep, send)
    n = w_qkv.shape[1]
    return enc[None], gin[None], grads[:, :n], grads[:, n:]


def solution(mesh):
    return jax.shard_map(
        shards,
        mesh=mesh,
        in_specs=(
            P("il", "xl", None, None),
            P("il", "xl", None, None),
            P("il", "xl"),
            P(("il", "xl"), None),
            P(("il", "xl"), None),
            P(),
        ),
        out_specs=(
            P("il", "xl", None, None),
            P("il", "xl", None, None),
            P(("il", "xl"), None),
            P(("il", "xl"), None),
        ),
        check_vma=False,
    )
```

```python
import functools

import jax
import jax.numpy as jnp
from jax import lax
from jax.experimental import pallas as pl
from jax.experimental.pallas import tpu as pltpu
from jax.sharding import PartitionSpec as P

HEAD_DIM = 64
HEADS = 6
D = 768
HD = 384
VMAX = 128
BLOCKS = 12
GROUP = 4
ROWS = GROUP * VMAX
BF16 = jnp.bfloat16
F32 = jnp.float32


def hop_x(v, k):
    return lax.ppermute(v, "il", [(i, (i // 4) * 4 + (i + k) % 4) for i in range(16)])


def hop_y(v, k):
    return lax.ppermute(v, "il", [(i, (i + 4 * k) % 16) for i in range(16)])


def hop_z(v, k):
    return lax.ppermute(v, "xl", [(i, (i + 2 * k) % 16) for i in range(16)])


def hop_core(v):
    return lax.ppermute(v, "xl", [(i, i ^ 1) for i in range(16)])


def coords():
    il = lax.axis_index("il")
    xl = lax.axis_index("xl")
    return il // 4, il % 4, xl // 2, xl % 2


def gather4(v, hop, direct):
    r1 = hop(v, -1)
    r3 = hop(v, 1)
    if direct:
        r2 = hop(v, 2)
    else:
        h = v.shape[0] // 2
        r2 = jnp.concatenate([hop(r1[:h], -1), hop(r3[h:], 1)], axis=0)
    return [v, r1, r2, r3]


def gather_weights(w):
    y, x, z, c = coords()
    n = w.shape[1] // 2
    mine = lax.dynamic_slice(w, (0, c * n), (3, n))
    other = lax.dynamic_slice(w, (0, (1 - c) * n), (3, n))
    block = jnp.concatenate([mine, hop_core(other), jnp.zeros((2, n), w.dtype)], axis=0)
    block = jnp.concatenate([block, lax.ppermute(block, "xl", [(i, i ^ 2) for i in range(16)])], axis=0)
    stack = jnp.concatenate([block, hop_z(block, 2), hop_z(block, -2), hop_z(block, 4)], axis=0)
    r = jnp.arange(48)[:, None]
    s = jnp.arange(64)[None, :]
    slot = s // 16
    j = s % 8
    origin = (z + jnp.where(slot == 3, 4, jnp.where(slot == 2, 2, jnp.where(slot == 1, 6, 0)))) % 8
    row = (origin ^ ((s // 8) % 2)) * 6 + (c ^ (j // 3)) * 3 + j % 3
    order = ((row == r) & (j < 6)).astype(w.dtype)
    v = jnp.dot(order, stack, preferred_element_type=F32).astype(w.dtype)
    v = jnp.concatenate(gather4(v, hop_x, True), axis=0)
    mine = gather4(v, hop_y, True)
    return mine + [hop_core(u) for u in mine]


def mm(a, b):
    return jnp.dot(a, b, preferred_element_type=F32)


def mm_t(a, b):
    return lax.dot_general(a, b, (((1,), (1,)), ((), ())), preferred_element_type=F32)


def tmm(a, b):
    return lax.dot_general(a, b, (((0,), (0,)), ((), ())), preferred_element_type=F32)


def norm_rows(xf):
    centred = xf - jnp.mean(xf, axis=-1, keepdims=True)
    inv = lax.rsqrt(jnp.mean(centred * centred, axis=-1, keepdims=True) + 1e-6)
    return centred * inv, inv


def row_mask(counts_ref, first, group):
    row_id = lax.broadcasted_iota(jnp.int32, (VMAX, D), 0)
    return jnp.concatenate([row_id < counts_ref[first + b] for b in range(group)], axis=0)


def core_kernel(*refs):
    at_ref, counts_ref = refs[:2]
    pieces = refs[2:10]
    x_ref, cot_ref, gain_ref = refs[10:13]
    w_out, att_out, gp_out, keep_out, send_out = refs[13:18]
    w_ref, nb_ref, go_ref, att_ref, gp_ref, keep_ref, send_ref, w_sems, row_sems, dw_sems = refs[18:]
    step = pl.program_id(0)
    last = pl.num_programs(0) - 1
    factor = HEAD_DIM**-0.5
    core = at_ref[2]

    @pl.when(step == 0)
    def _():
        y, x = at_ref[0], at_ref[1]
        copies = []
        for rel in range(2):
            half = core ^ rel
            for ky in range(4):
                for kx in range(4):
                    row = pl.multiple_of(((y + ky) & 3) * 192 + ((x + kx) & 3) * 48, 16)
                    copies.append(
                        pltpu.make_async_copy(
                            pieces[rel * 4 + ky].at[pl.ds(kx * 48, 48), :],
                            w_ref.at[half, pl.ds(row, 48), :],
                            w_sems.at[len(copies)],
                        )
                    )
        for copy in copies:
            copy.start()
        for copy in copies:
            copy.wait()

    whole_w = pltpu.make_async_copy(w_ref, w_out, w_sems.at[32])

    @pl.when(step == 0)
    def _():
        whole_w.start()

    normed, _ = norm_rows(x_ref[...].reshape(ROWS, D).astype(F32))
    nb = (normed * gain_ref[...]).astype(BF16)
    mask = row_mask(counts_ref, step * GROUP, GROUP)
    go = jnp.where(mask, cot_ref[...].reshape(ROWS, D).astype(F32), 0.0).astype(BF16)
    at = pl.ds(pl.multiple_of(step * ROWS, ROWS), ROWS)
    nb_ref[at, :] = nb
    go_ref[at, :] = go

    qk = mm(nb, w_ref[0]).astype(BF16)
    vv = mm(nb, w_ref[1, :, :HD]).astype(BF16)
    ga = mm(go, w_ref[1, :, HD:]).astype(BF16)
    key_id = lax.broadcasted_iota(jnp.int32, (VMAX, 2 * VMAX), 0)
    lane = lax.broadcasted_iota(jnp.int32, (1, 2 * HEAD_DIM), 1)
    first = jnp.where(lane < HEAD_DIM, 1.0, 0.0)
    m0, m1 = first.astype(BF16), (1.0 - first).astype(BF16)
    f0, f1 = (first * factor).astype(BF16), ((1.0 - first) * factor).astype(BF16)
    pair = lambda a, u, w: jnp.concatenate([a * u, a * w], axis=0)
    stack = lambda a: jnp.concatenate([a[:, :VMAX], a[:, VMAX:]], axis=0)
    for b in range(GROUP):
        live = key_id < counts_ref[step * GROUP + b]
        rs = slice(b * VMAX, (b + 1) * VMAX)
        at_b = pl.ds(pl.multiple_of(step * ROWS + b * VMAX, VMAX), VMAX)
        for lo in range(0, HD, 2 * HEAD_DIM):
            hi = lo + 2 * HEAD_DIM
            k = qk[rs, HD + lo : HD + hi]
            v = vv[rs, lo:hi]
            q2 = pair(qk[rs, lo:hi], f0, f1)
            g2 = pair(ga[rs, lo:hi], m0, m1)
            s = jnp.where(live, mm_t(k, q2), -1e30)
            e = jnp.exp(s - jnp.max(s, axis=0, keepdims=True))
            p = e * (1.0 / jnp.sum(e, axis=0, keepdims=True))
            pb = p.astype(BF16)
            dp = mm_t(v, g2)
            ds = (p * (dp - jnp.sum(p * dp, axis=0, keepdims=True))).astype(BF16)
            att_ref[at_b, lo:hi] = tmm(stack(pb), pair(v, m0, m1)).astype(BF16)
            gp_ref[at_b, lo:hi] = tmm(stack(ds), pair(k, f0, f1)).astype(BF16)
            gp_ref[at_b, HD + lo : HD + hi] = mm(ds, q2).astype(BF16)
            gp_ref[at_b, D + lo : D + hi] = mm(pb, g2).astype(BF16)

    def row_copies(i):
        rows = pl.ds(pl.multiple_of(i * ROWS, ROWS), ROWS)
        return (
            pltpu.make_async_copy(att_ref.at[rows, :], att_out.at[rows, :], row_sems.at[0, i]),
            pltpu.make_async_copy(gp_ref.at[rows, :], gp_out.at[rows, :], row_sems.at[1, i]),
        )

    for copy in row_copies(step):
        copy.start()

    @pl.when(step == last)
    def _():
        copies = []
        for i in range(D // 256):
            rr = slice(i * 256, i * 256 + 256)
            gw = tmm(nb_ref[:, rr], gp_ref[...])
            for half, cols, val in (
                (0, slice(0, D), gw[:, :D]),
                (1, slice(0, HD), gw[:, D:]),
                (1, slice(HD, D), tmm(go_ref[:, rr], att_ref[...])),
            ):

                @pl.when(core == half)
                def _():
                    keep_ref[rr, cols] = val

                @pl.when(core != half)
                def _():
                    send_ref[rr, cols] = val.astype(send_ref.dtype)

            copies.append(pltpu.make_async_copy(keep_ref.at[rr, :], keep_out.at[rr, :], dw_sems.at[0, i]))
            copies.append(pltpu.make_async_copy(send_ref.at[rr, :], send_out.at[rr, :], dw_sems.at[1, i]))
            copies[-1].start()
            copies[-2].start()
        whole_w.wait()
        for i in range(BLOCKS // GROUP):
            for copy in row_copies(i):
                copy.wait()
        for copy in copies:
            copy.wait()


def grads_core(at, counts, pieces, tiles, cotan, gain):
    nblock = tiles.shape[0]
    rows = nblock * VMAX
    hbm = pl.BlockSpec(memory_space=pltpu.HBM)
    tile = pl.BlockSpec((GROUP, VMAX, D), lambda i, *_: (i, 0, 0))
    return pl.pallas_call(
        core_kernel,
        grid_spec=pltpu.PrefetchScalarGridSpec(
            num_scalar_prefetch=2,
            grid=(nblock // GROUP,),
            in_specs=[hbm] * 8 + [tile, tile, pl.BlockSpec((1, D), lambda i, *_: (0, 0))],
            out_specs=[hbm] * 3 + [pl.BlockSpec(memory_space=pl.ANY)] * 2,
            scratch_shapes=[
                pltpu.VMEM((2, D, D), BF16),
                pltpu.VMEM((rows, D), BF16),
                pltpu.VMEM((rows, D), BF16),
                pltpu.VMEM((rows, HD), BF16),
                pltpu.VMEM((rows, 3 * HD), BF16),
                pltpu.VMEM((D, D), F32),
                pltpu.VMEM((D, D), BF16),
                pltpu.SemaphoreType.DMA((33,)),
                pltpu.SemaphoreType.DMA((2, nblock // GROUP)),
                pltpu.SemaphoreType.DMA((2, D // 256)),
            ],
        ),
        out_shape=[
            jax.ShapeDtypeStruct((2, D, D), BF16),
            jax.ShapeDtypeStruct((rows, HD), BF16),
            jax.ShapeDtypeStruct((rows, 3 * HD), BF16),
            jax.ShapeDtypeStruct((D, D), F32),
            jax.ShapeDtypeStruct((D, D), BF16),
        ],
        compiler_params=pltpu.CompilerParams(
            dimension_semantics=("arbitrary",), vmem_limit_bytes=28 * 1024 * 1024
        ),
        cost_estimate=pl.CostEstimate(flops=20_000_000_000, bytes_accessed=18_000_000, transcendentals=1_200_000),
    )(at, counts, *pieces, tiles, cotan, gain)


def rows_kernel(first, counts_ref, w_ref, att_ref, gp_ref, x_ref, cot_ref, gain_ref, *rest):
    enc_ref, gin_ref = rest[-2:]
    gain = gain_ref[...]
    xf = x_ref[...].reshape(ROWS, D).astype(F32)
    normed, inv = norm_rows(xf)
    mask = row_mask(counts_ref, (first + pl.program_id(0)) * GROUP, GROUP)
    enc = xf + mm_t(att_ref[...], w_ref[1, :, HD:])
    enc_ref[...] = jnp.where(mask, enc, 0.0).astype(BF16).reshape(GROUP, VMAX, D)
    gp = gp_ref[...]
    gn = (mm_t(gp[:, :D], w_ref[0]) + mm_t(gp[:, D:], w_ref[1, :, :HD])) * gain
    gl = inv * (
        gn - jnp.mean(gn, axis=-1, keepdims=True) - normed * jnp.mean(gn * normed, axis=-1, keepdims=True)
    )
    gin = cot_ref[...].reshape(ROWS, D).astype(F32) + gl
    gin_ref[...] = jnp.where(mask, gin, 0.0).astype(BF16).reshape(GROUP, VMAX, D)


def rows_part(first, count, counts, w, att, gp, tiles, cotan, gain, done):
    tile = pl.BlockSpec((GROUP, VMAX, D), lambda i, *_: (i + first, 0, 0))
    flat = lambda cols: pl.BlockSpec((ROWS, cols), lambda i, *_: (i + first, 0))
    return pl.pallas_call(
        functools.partial(rows_kernel, first),
        grid_spec=pltpu.PrefetchScalarGridSpec(
            num_scalar_prefetch=1,
            grid=(count,),
            in_specs=[
                pl.BlockSpec((2, D, D), lambda i, *_: (0, 0, 0), pipeline_mode=pl.Buffered(1)),
                flat(HD),
                flat(3 * HD),
                tile,
                tile,
                pl.BlockSpec((1, D), lambda i, *_: (0, 0)),
            ]
            + [pl.BlockSpec(memory_space=pl.ANY)] * len(done),
            out_specs=[tile, tile],
        ),
        out_shape=[jax.ShapeDtypeStruct(tiles.shape, BF16)] * 2,
        input_output_aliases={7 + i: i for i in range(len(done))},
        compiler_params=pltpu.CompilerParams(
            dimension_semantics=("arbitrary",), vmem_limit_bytes=60 * 1024 * 1024
        ),
        cost_estimate=pl.CostEstimate(
            flops=count * 1_300_000_000, bytes_accessed=count * 5_000_000, transcendentals=1000
        ),
    )(counts, w, att, gp, tiles, cotan, gain, *done)


def small_call(kernel, at, args, outs):
    smem = [] if at is None else [pl.BlockSpec(memory_space=pltpu.SMEM)]
    vmem = pl.BlockSpec(memory_space=pltpu.VMEM)
    size = sum(a.size * a.dtype.itemsize for a in args)
    return pl.pallas_call(
        kernel,
        in_specs=smem + [vmem] * len(args),
        out_specs=[vmem] * len(outs),
        out_shape=[jax.ShapeDtypeStruct(shape, dtype) for shape, dtype in outs],
        compiler_params=pltpu.CompilerParams(vmem_limit_bytes=12 * 1024 * 1024),
        cost_estimate=pl.CostEstimate(flops=size, bytes_accessed=2 * size, transcendentals=0),
    )(*([] if at is None else [at]), *args)


def cut_kernel(axis, at_ref, own_ref, *refs):
    got, outs = refs[:-4], refs[-4:]
    rows = outs[0].shape[0]
    for k in range(4):
        at = pl.ds(pl.multiple_of(((at_ref[axis] + k) & 3) * rows, rows), rows)
        total = own_ref[at, :]
        for ref in got:
            total = total + ref[at, :].astype(F32)
        outs[k][...] = total.astype(outs[k].dtype)


def cut(at, axis, own, *got):
    rows, n = own.shape[0] // 4, own.shape[1]
    outs = [((rows, n), F32)] + [((rows, n), BF16)] * 3
    return small_call(functools.partial(cut_kernel, axis), at, [own, *got], outs)


def triples_kernel(own_ref, *refs):
    total = own_ref[...]
    for ref in refs[:-1]:
        total = total + ref[...].astype(F32)
    for i in range(16):
        refs[-1][i] = total[3 * i : 3 * i + 3, :]


def finish_kernel(got_ref, qkv_ref, out_ref):
    lo, hi = got_ref[0], got_ref[1]
    for z in range(1, 8):
        lo = lo + got_ref[2 * z]
        hi = hi + got_ref[2 * z + 1]
    qkv_ref[:, :D] = lo
    qkv_ref[:, D:] = hi[:, :HD]
    out_ref[...] = hi[:, HD:]


def scatter_grads(at, keep, send):
    own, *out = cut(at, 0, keep, hop_core(send))
    own, *out = cut(at, 1, own, *[hop_y(v, k + 1) for k, v in enumerate(out)])
    parts = [own] + [hop_x(v, k + 1) for k, v in enumerate(out)]
    n = keep.shape[1]
    (v,) = small_call(triples_kernel, None, parts, [((16, 3, n), F32)])
    got = lax.all_to_all(v, "xl", split_axis=0, concat_axis=0, tiled=True)
    return small_call(finish_kernel, None, [got], [((3, n + n // 2), F32), ((3, n // 2), F32)])


def shards(patches, out_cot, vis_count, w_qkv, w_out, ln_gain):
    y, x, z, c = coords()
    pieces = gather_weights(jnp.concatenate([w_qkv, w_out], axis=1))
    at = jnp.stack([y, x, c]).astype(jnp.int32)
    counts, tiles, cotan, gain = vis_count[0], patches[0], out_cot[0], ln_gain[None]
    w, att, gp, keep, send = grads_core(at, counts, pieces, tiles, cotan, gain)
    out = rows_part(0, 1, counts, w, att, gp, tiles, cotan, gain, ())
    enc, gin = rows_part(1, 2, counts, w, att, gp, tiles, cotan, gain, out)
    grad_qkv, grad_out = scatter_grads(at, keep, send)
    return enc[None], gin[None], grad_qkv, grad_out


def solution(mesh):
    return jax.shard_map(
        shards,
        mesh=mesh,
        in_specs=(
            P("il", "xl", None, None),
            P("il", "xl", None, None),
            P("il", "xl"),
            P(("il", "xl"), None),
            P(("il", "xl"), None),
            P(),
        ),
        out_specs=(
            P("il", "xl", None, None),
            P("il", "xl", None, None),
            P(("il", "xl"), None),
            P(("il", "xl"), None),
        ),
        check_vma=False,
    )
```

```python
import functools

import jax
import jax.numpy as jnp
from jax import lax
from jax.experimental import pallas as pl
from jax.experimental.pallas import tpu as pltpu
from jax.sharding import PartitionSpec as P

HEAD_DIM = 64
HEADS = 6
D = 768
HD = 384
VMAX = 128
BLOCKS = 12
GROUP = 4
ROWS = GROUP * VMAX
PRE = 2
TAIL = 2
NORM_MIB = 60
CORE_MIB = 44
TAIL_MIB = 60
BF16 = jnp.bfloat16
F32 = jnp.float32


def hop_x(v, k):
    return lax.ppermute(v, "il", [(i, (i // 4) * 4 + (i + k) % 4) for i in range(16)])


def hop_y(v, k):
    return lax.ppermute(v, "il", [(i, (i + 4 * k) % 16) for i in range(16)])


def hop_z(v, k):
    return lax.ppermute(v, "xl", [(i, (i + 2 * k) % 16) for i in range(16)])


def hop_core(v):
    return lax.ppermute(v, "xl", [(i, i ^ 1) for i in range(16)])


def coords():
    il = lax.axis_index("il")
    xl = lax.axis_index("xl")
    return il // 4, il % 4, xl // 2, xl % 2


def gather4(v, hop, direct):
    r1 = hop(v, -1)
    r3 = hop(v, 1)
    if direct:
        r2 = hop(v, 2)
    else:
        h = v.shape[0] // 2
        r2 = jnp.concatenate([hop(r1[:h], -1), hop(r3[h:], 1)], axis=0)
    return [v, r1, r2, r3]


def gather_weights(w, during):
    y, x, z, c = coords()
    n = w.shape[1] // 2
    mine = lax.dynamic_slice(w, (0, c * n), (3, n))
    other = lax.dynamic_slice(w, (0, (1 - c) * n), (3, n))
    block = jnp.concatenate([mine, hop_core(other), jnp.zeros((2, n), w.dtype)], axis=0)
    block = jnp.concatenate([block, lax.ppermute(block, "xl", [(i, i ^ 2) for i in range(16)])], axis=0)
    stack = jnp.concatenate([block, hop_z(block, 2), hop_z(block, -2), hop_z(block, 4)], axis=0)
    r = jnp.arange(48)[:, None]
    s = jnp.arange(64)[None, :]
    slot = s // 16
    j = s % 8
    origin = (z + jnp.where(slot == 3, 4, jnp.where(slot == 2, 2, jnp.where(slot == 1, 6, 0)))) % 8
    row = (origin ^ ((s // 8) % 2)) * 6 + (c ^ (j // 3)) * 3 + j % 3
    order = ((row == r) & (j < 6)).astype(w.dtype)
    v = jnp.dot(order, stack, preferred_element_type=F32).astype(w.dtype)
    v = jnp.concatenate(gather4(v, hop_x, True), axis=0)
    mine = gather4(v, hop_y, True)
    extra = during(v)
    mine[1], extra = lax.optimization_barrier((mine[1], extra))
    return mine + [hop_core(u) for u in mine], extra


def mm(a, b):
    return jnp.dot(a, b, preferred_element_type=F32)


def mm_t(a, b):
    return lax.dot_general(a, b, (((1,), (1,)), ((), ())), preferred_element_type=F32)


def tmm(a, b):
    return lax.dot_general(a, b, (((0,), (0,)), ((), ())), preferred_element_type=F32)


def norm_rows(xf):
    centred = xf - jnp.mean(xf, axis=-1, keepdims=True)
    inv = lax.rsqrt(jnp.mean(centred * centred, axis=-1, keepdims=True) + 1e-6)
    return centred * inv, inv


def row_mask(counts_ref, first, group):
    row_id = lax.broadcasted_iota(jnp.int32, (VMAX, D), 0)
    return jnp.concatenate([row_id < counts_ref[first + b] for b in range(group)], axis=0)


def norm_kernel(counts_ref, x_ref, cot_ref, gain_ref, nb_ref, go_ref):
    rows = PRE * VMAX
    normed, _ = norm_rows(x_ref[...].reshape(rows, D).astype(F32))
    nb_ref[...] = (normed * gain_ref[...]).astype(BF16)
    mask = row_mask(counts_ref, pl.program_id(0) * PRE, PRE)
    go_ref[...] = jnp.where(mask, cot_ref[...].reshape(rows, D).astype(F32), 0.0).astype(BF16)


def norm_part(counts, tiles, cotan, gain):
    nblock = tiles.shape[0]
    tile = pl.BlockSpec((PRE, VMAX, D), lambda i, *_: (i, 0, 0))
    flat = pl.BlockSpec((PRE * VMAX, D), lambda i, *_: (i, 0))
    return pl.pallas_call(
        norm_kernel,
        grid_spec=pltpu.PrefetchScalarGridSpec(
            num_scalar_prefetch=1,
            grid=(nblock // PRE,),
            in_specs=[tile, tile, pl.BlockSpec((1, D), lambda i, *_: (0, 0))],
            out_specs=[flat, flat],
        ),
        out_shape=[jax.ShapeDtypeStruct((nblock * VMAX, D), BF16)] * 2,
        compiler_params=pltpu.CompilerParams(
            dimension_semantics=("arbitrary",), vmem_limit_bytes=NORM_MIB * 1024 * 1024
        ),
        cost_estimate=pl.CostEstimate(flops=20_000_000, bytes_accessed=9_500_000, transcendentals=2000),
    )(counts, tiles, cotan, gain)


def core_kernel(*refs):
    at_ref, counts_ref = refs[:2]
    pieces = refs[2:10]
    nb_in, go_in = refs[10:12]
    w_out, att_out, gp_out, keep_out, send_out = refs[12:17]
    w_ref, nb_ref, go_ref, att_ref, gp_ref, keep_ref, send_ref, w_sems, row_sems, dw_sems = refs[17:]
    step = pl.program_id(0)
    last = pl.num_programs(0) - 1
    factor = HEAD_DIM**-0.5
    core = at_ref[2]

    @pl.when(step == 0)
    def _():
        y, x = at_ref[0], at_ref[1]
        copies = []
        for rel in range(2):
            half = core ^ rel
            for ky in range(4):
                for kx in range(4):
                    row = pl.multiple_of(((y + ky) & 3) * 192 + ((x + kx) & 3) * 48, 16)
                    copies.append(
                        pltpu.make_async_copy(
                            pieces[rel * 4 + ky].at[pl.ds(kx * 48, 48), :],
                            w_ref.at[half, pl.ds(row, 48), :],
                            w_sems.at[len(copies)],
                        )
                    )
        for copy in copies:
            copy.start()
        for copy in copies:
            copy.wait()

    whole_w = pltpu.make_async_copy(w_ref, w_out, w_sems.at[32])

    @pl.when(step == 0)
    def _():
        whole_w.start()

    nb, go = nb_in[...], go_in[...]
    at = pl.ds(pl.multiple_of(step * ROWS, ROWS), ROWS)
    nb_ref[at, :] = nb
    go_ref[at, :] = go

    qk = mm(nb, w_ref[0]).astype(BF16)
    vv = mm(nb, w_ref[1, :, :HD]).astype(BF16)
    ga = mm(go, w_ref[1, :, HD:]).astype(BF16)
    key_id = lax.broadcasted_iota(jnp.int32, (VMAX, 2 * VMAX), 0)
    lane = lax.broadcasted_iota(jnp.int32, (1, 2 * HEAD_DIM), 1)
    first = jnp.where(lane < HEAD_DIM, 1.0, 0.0)
    m0, m1 = first.astype(BF16), (1.0 - first).astype(BF16)
    f0, f1 = (first * factor).astype(BF16), ((1.0 - first) * factor).astype(BF16)
    pair = lambda a, u, w: jnp.concatenate([a * u, a * w], axis=0)
    stack = lambda a: jnp.concatenate([a[:, :VMAX], a[:, VMAX:]], axis=0)
    for b in range(GROUP):
        live = key_id < counts_ref[step * GROUP + b]
        rs = slice(b * VMAX, (b + 1) * VMAX)
        at_b = pl.ds(pl.multiple_of(step * ROWS + b * VMAX, VMAX), VMAX)
        for lo in range(0, HD, 2 * HEAD_DIM):
            hi = lo + 2 * HEAD_DIM
            k = qk[rs, HD + lo : HD + hi]
            v = vv[rs, lo:hi]
            q2 = pair(qk[rs, lo:hi], f0, f1)
            g2 = pair(ga[rs, lo:hi], m0, m1)
            s = jnp.where(live, mm_t(k, q2), -1e30)
            e = jnp.exp(s - jnp.max(s, axis=0, keepdims=True))
            p = e * (1.0 / jnp.sum(e, axis=0, keepdims=True))
            pb = p.astype(BF16)
            dp = mm_t(v, g2)
            ds = (p * (dp - jnp.sum(p * dp, axis=0, keepdims=True))).astype(BF16)
            att_ref[at_b, lo:hi] = tmm(stack(pb), pair(v, m0, m1)).astype(BF16)
            gp_ref[at_b, lo:hi] = tmm(stack(ds), pair(k, f0, f1)).astype(BF16)
            gp_ref[at_b, HD + lo : HD + hi] = mm(ds, q2).astype(BF16)
            gp_ref[at_b, D + lo : D + hi] = mm(pb, g2).astype(BF16)

    def row_copies(i):
        rows = pl.ds(pl.multiple_of(i * ROWS, ROWS), ROWS)
        return (
            pltpu.make_async_copy(att_ref.at[rows, :], att_out.at[rows, :], row_sems.at[0, i]),
            pltpu.make_async_copy(gp_ref.at[rows, :], gp_out.at[rows, :], row_sems.at[1, i]),
        )

    for copy in row_copies(step):
        copy.start()

    @pl.when(step == last)
    def _():
        copies = []
        for i in range(D // 256):
            rr = slice(i * 256, i * 256 + 256)
            gw = tmm(nb_ref[:, rr], gp_ref[...])
            for half, cols, val in (
                (0, slice(0, D), gw[:, :D]),
                (1, slice(0, HD), gw[:, D:]),
                (1, slice(HD, D), tmm(go_ref[:, rr], att_ref[...])),
            ):

                @pl.when(core == half)
                def _():
                    keep_ref[rr, cols] = val

                @pl.when(core != half)
                def _():
                    send_ref[rr, cols] = val.astype(send_ref.dtype)

            copies.append(pltpu.make_async_copy(keep_ref.at[rr, :], keep_out.at[rr, :], dw_sems.at[0, i]))
            copies.append(pltpu.make_async_copy(send_ref.at[rr, :], send_out.at[rr, :], dw_sems.at[1, i]))
            copies[-1].start()
            copies[-2].start()
        whole_w.wait()
        for i in range(BLOCKS // GROUP):
            for copy in row_copies(i):
                copy.wait()
        for copy in copies:
            copy.wait()


def grads_core(at, counts, pieces, nb, go):
    rows = nb.shape[0]
    nblock = rows // VMAX
    hbm = pl.BlockSpec(memory_space=pltpu.HBM)
    tile = pl.BlockSpec((ROWS, D), lambda i, *_: (i, 0))
    return pl.pallas_call(
        core_kernel,
        grid_spec=pltpu.PrefetchScalarGridSpec(
            num_scalar_prefetch=2,
            grid=(nblock // GROUP,),
            in_specs=[hbm] * 8 + [tile, tile],
            out_specs=[hbm] * 3 + [pl.BlockSpec(memory_space=pl.ANY)] * 2,
            scratch_shapes=[
                pltpu.VMEM((2, D, D), BF16),
                pltpu.VMEM((rows, D), BF16),
                pltpu.VMEM((rows, D), BF16),
                pltpu.VMEM((rows, HD), BF16),
                pltpu.VMEM((rows, 3 * HD), BF16),
                pltpu.VMEM((D, D), F32),
                pltpu.VMEM((D, D), BF16),
                pltpu.SemaphoreType.DMA((33,)),
                pltpu.SemaphoreType.DMA((2, nblock // GROUP)),
                pltpu.SemaphoreType.DMA((2, D // 256)),
            ],
        ),
        out_shape=[
            jax.ShapeDtypeStruct((2, D, D), BF16),
            jax.ShapeDtypeStruct((rows, HD), BF16),
            jax.ShapeDtypeStruct((rows, 3 * HD), BF16),
            jax.ShapeDtypeStruct((D, D), F32),
            jax.ShapeDtypeStruct((D, D), BF16),
        ],
        compiler_params=pltpu.CompilerParams(
            dimension_semantics=("arbitrary",), vmem_limit_bytes=CORE_MIB * 1024 * 1024
        ),
        cost_estimate=pl.CostEstimate(flops=20_000_000_000, bytes_accessed=18_000_000, transcendentals=1_200_000),
    )(at, counts, *pieces, nb, go)


def rows_kernel(counts_ref, w_ref, att_ref, gp_ref, x_ref, cot_ref, gain_ref, enc_ref, gin_ref):
    gain = gain_ref[...]
    xf = x_ref[...].reshape(TAIL * VMAX, D).astype(F32)
    normed, inv = norm_rows(xf)
    mask = row_mask(counts_ref, pl.program_id(0) * TAIL, TAIL)
    enc = xf + mm_t(att_ref[...], w_ref[1, :, HD:])
    enc_ref[...] = jnp.where(mask, enc, 0.0).astype(BF16).reshape(TAIL, VMAX, D)
    gp = gp_ref[...]
    gn = (mm_t(gp[:, :D], w_ref[0]) + mm_t(gp[:, D:], w_ref[1, :, :HD])) * gain
    gl = inv * (
        gn - jnp.mean(gn, axis=-1, keepdims=True) - normed * jnp.mean(gn * normed, axis=-1, keepdims=True)
    )
    gin = cot_ref[...].reshape(TAIL * VMAX, D).astype(F32) + gl
    gin_ref[...] = jnp.where(mask, gin, 0.0).astype(BF16).reshape(TAIL, VMAX, D)


def rows_part(counts, w, att, gp, tiles, cotan, gain):
    nblock = tiles.shape[0]
    tile = pl.BlockSpec((TAIL, VMAX, D), lambda i, *_: (i, 0, 0))
    flat = lambda cols: pl.BlockSpec((TAIL * VMAX, cols), lambda i, *_: (i, 0))
    return pl.pallas_call(
        rows_kernel,
        grid_spec=pltpu.PrefetchScalarGridSpec(
            num_scalar_prefetch=1,
            grid=(nblock // TAIL,),
            in_specs=[
                pl.BlockSpec((2, D, D), lambda i, *_: (0, 0, 0), pipeline_mode=pl.Buffered(1)),
                flat(HD),
                flat(3 * HD),
                tile,
                tile,
                pl.BlockSpec((1, D), lambda i, *_: (0, 0)),
            ],
            out_specs=[tile, tile],
        ),
        out_shape=[jax.ShapeDtypeStruct(tiles.shape, BF16)] * 2,
        compiler_params=pltpu.CompilerParams(
            dimension_semantics=("arbitrary",), vmem_limit_bytes=TAIL_MIB * 1024 * 1024
        ),
        cost_estimate=pl.CostEstimate(flops=4_000_000_000, bytes_accessed=16_000_000, transcendentals=3000),
    )(counts, w, att, gp, tiles, cotan, gain)


def small_call(kernel, at, args, outs):
    smem = [] if at is None else [pl.BlockSpec(memory_space=pltpu.SMEM)]
    vmem = pl.BlockSpec(memory_space=pltpu.VMEM)
    size = sum(a.size * a.dtype.itemsize for a in args)
    return pl.pallas_call(
        kernel,
        in_specs=smem + [vmem] * len(args),
        out_specs=[vmem] * len(outs),
        out_shape=[jax.ShapeDtypeStruct(shape, dtype) for shape, dtype in outs],
        compiler_params=pltpu.CompilerParams(vmem_limit_bytes=12 * 1024 * 1024),
        cost_estimate=pl.CostEstimate(flops=size, bytes_accessed=2 * size, transcendentals=0),
    )(*([] if at is None else [at]), *args)


def first_cut_kernel(at_ref, keep_ref, got_ref, *outs):
    for k in range(4):
        at = pl.ds(pl.multiple_of(((at_ref[0] + k) & 3) * 192, 192), 192)
        outs[k][...] = (keep_ref[at, :HD] + got_ref[at, :HD].astype(F32)).astype(outs[k].dtype)
        for j in range(4):
            at = pl.ds(pl.multiple_of(j * 192 + ((at_ref[1] + k) & 3) * 48, 48), 48)
            part = keep_ref[at, HD:] + got_ref[at, HD:].astype(F32)
            outs[4 + k][j * 48 : j * 48 + 48, :] = part.astype(outs[4 + k].dtype)


def next_cut_kernel(at_ref, *refs):
    ins, outs = refs[:8], refs[8:]
    for side in range(2):
        for k in range(4):
            at = pl.ds(pl.multiple_of(((at_ref[1 - side] + k) & 3) * 48, 48), 48)
            total = ins[4 * side][at, :]
            for ref in ins[4 * side + 1 : 4 * side + 4]:
                total = total + ref[at, :].astype(F32)
            outs[4 * side + k][...] = total.astype(outs[4 * side + k].dtype)


def triples_kernel(*refs):
    for side in range(2):
        total = refs[4 * side][...]
        for ref in refs[4 * side + 1 : 4 * side + 4]:
            total = total + ref[...].astype(F32)
        for i in range(16):
            refs[-1][i, :, side * HD : side * HD + HD] = total[3 * i : 3 * i + 3, :]


def finish_kernel(got_ref, qkv_ref, out_ref):
    lo, hi = got_ref[0], got_ref[1]
    for z in range(1, 8):
        lo = lo + got_ref[2 * z]
        hi = hi + got_ref[2 * z + 1]
    qkv_ref[:, :D] = lo
    qkv_ref[:, D:] = hi[:, :HD]
    out_ref[...] = hi[:, HD:]


def scatter_grads(at, keep, send):
    n = keep.shape[1]
    slots = lambda rows: ([((rows, HD), F32)] + [((rows, HD), BF16)] * 3) * 2
    v = small_call(first_cut_kernel, at, [keep, hop_core(send)], slots(192))
    left = [v[0]] + [hop_y(v[k], k) for k in (1, 3, 2)]
    right = [v[4]] + [hop_x(v[4 + k], k) for k in (1, 3, 2)]
    v = small_call(next_cut_kernel, at, left + right, slots(48))
    left = [v[0]] + [hop_x(v[k], k) for k in (1, 3, 2)]
    right = [v[4]] + [hop_y(v[4 + k], k) for k in (1, 3, 2)]
    (v,) = small_call(triples_kernel, None, left + right, [((16, 3, n), F32)])
    got = lax.all_to_all(v, "xl", split_axis=0, concat_axis=0, tiled=True)
    return small_call(finish_kernel, None, [got], [((3, n + n // 2), F32), ((3, n // 2), F32)])


def shards(patches, out_cot, vis_count, w_qkv, w_out, ln_gain):
    y, x, z, c = coords()
    at = jnp.stack([y, x, c]).astype(jnp.int32)
    counts, tiles, cotan, gain = vis_count[0], patches[0], out_cot[0], ln_gain[None]

    def during(v):
        late, _ = lax.optimization_barrier((counts, v))
        return norm_part(late, tiles, cotan, gain)

    pieces, (nb, go) = gather_weights(jnp.concatenate([w_qkv, w_out], axis=1), during)
    w, att, gp, keep, send = grads_core(at, counts, pieces, nb, go)
    enc, gin = rows_part(counts, w, att, gp, tiles, cotan, gain)
    grad_qkv, grad_out = scatter_grads(at, keep, send)
    return enc[None], gin[None], grad_qkv, grad_out


def solution(mesh):
    return jax.shard_map(
        shards,
        mesh=mesh,
        in_specs=(
            P("il", "xl", None, None),
            P("il", "xl", None, None),
            P("il", "xl"),
            P(("il", "xl"), None),
            P(("il", "xl"), None),
            P(),
        ),
        out_specs=(
            P("il", "xl", None, None),
            P("il", "xl", None, None),
            P(("il", "xl"), None),
            P(("il", "xl"), None),
        ),
        check_vma=False,
    )
```

```python
import functools

import jax
import jax.numpy as jnp
from jax import lax
from jax.experimental import pallas as pl
from jax.experimental.pallas import tpu as pltpu
from jax.sharding import PartitionSpec as P

HEAD_DIM = 64
HEADS = 6
D = 768
HD = 384
VMAX = 128
BLOCKS = 12
GROUP = 4
ROWS = GROUP * VMAX
TAIL = 2
HEAD = 3
NORM_MIB = 0
CORE_MIB = 51
TAIL_MIB = 60
BF16 = jnp.bfloat16
F32 = jnp.float32


def hop_x(v, k):
    return lax.ppermute(v, "il", [(i, (i // 4) * 4 + (i + k) % 4) for i in range(16)])


def hop_y(v, k):
    return lax.ppermute(v, "il", [(i, (i + 4 * k) % 16) for i in range(16)])


def hop_z(v, k):
    return lax.ppermute(v, "xl", [(i, (i + 2 * k) % 16) for i in range(16)])


def hop_core(v):
    return lax.ppermute(v, "xl", [(i, i ^ 1) for i in range(16)])


def coords():
    il = lax.axis_index("il")
    xl = lax.axis_index("xl")
    return il // 4, il % 4, xl // 2, xl % 2


def gather4(v, hop, direct):
    r1 = hop(v, -1)
    r3 = hop(v, 1)
    if direct:
        r2 = hop(v, 2)
    else:
        h = v.shape[0] // 2
        r2 = jnp.concatenate([hop(r1[:h], -1), hop(r3[h:], 1)], axis=0)
    return [v, r1, r2, r3]


def gather_weights(w):
    y, x, z, c = coords()
    n = w.shape[1] // 2
    mine = lax.dynamic_slice(w, (0, c * n), (3, n))
    other = lax.dynamic_slice(w, (0, (1 - c) * n), (3, n))
    block = jnp.concatenate([mine, hop_core(other), jnp.zeros((2, n), w.dtype)], axis=0)
    block = jnp.concatenate([block, lax.ppermute(block, "xl", [(i, i ^ 2) for i in range(16)])], axis=0)
    stack = jnp.concatenate([block, hop_z(block, 2), hop_z(block, -2), hop_z(block, 4)], axis=0)
    r = jnp.arange(48)[:, None]
    s = jnp.arange(64)[None, :]
    slot = s // 16
    j = s % 8
    origin = (z + jnp.where(slot == 3, 4, jnp.where(slot == 2, 2, jnp.where(slot == 1, 6, 0)))) % 8
    row = (origin ^ ((s // 8) % 2)) * 6 + (c ^ (j // 3)) * 3 + j % 3
    order = ((row == r) & (j < 6)).astype(w.dtype)
    v = jnp.dot(order, stack, preferred_element_type=F32).astype(w.dtype)
    v = jnp.concatenate(gather4(v, hop_x, True), axis=0)
    mine = gather4(v, hop_y, True)
    return mine + [hop_core(u) for u in mine]


def mm(a, b):
    return jnp.dot(a, b, preferred_element_type=F32)


def mm_t(a, b):
    return lax.dot_general(a, b, (((1,), (1,)), ((), ())), preferred_element_type=F32)


def tmm(a, b):
    return lax.dot_general(a, b, (((0,), (0,)), ((), ())), preferred_element_type=F32)


def norm_rows(xf):
    centred = xf - jnp.mean(xf, axis=-1, keepdims=True)
    inv = lax.rsqrt(jnp.mean(centred * centred, axis=-1, keepdims=True) + 1e-6)
    return centred * inv, inv


def row_mask(counts_ref, first, group):
    row_id = lax.broadcasted_iota(jnp.int32, (VMAX, D), 0)
    return jnp.concatenate([row_id < counts_ref[first + b] for b in range(group)], axis=0)


def core_kernel(*refs):
    at_ref, counts_ref = refs[:2]
    pieces = refs[2:10]
    x_ref, cot_ref, gain_ref = refs[10:13]
    w_out, att_out, gp_out, keep_out, send_out = refs[13:18]
    w_ref, nb_ref, go_ref, att_ref, gp_ref, keep_ref, send_ref, w_sems, row_sems, dw_sems = refs[18:]
    step = pl.program_id(0)
    last = pl.num_programs(0) - 1
    factor = HEAD_DIM**-0.5
    core = at_ref[2]

    @pl.when(step == 0)
    def _():
        y, x = at_ref[0], at_ref[1]
        copies = []
        for rel in range(2):
            half = core ^ rel
            for ky in range(4):
                for kx in range(4):
                    row = pl.multiple_of(((y + ky) & 3) * 192 + ((x + kx) & 3) * 48, 16)
                    copies.append(
                        pltpu.make_async_copy(
                            pieces[rel * 4 + ky].at[pl.ds(kx * 48, 48), :],
                            w_ref.at[half, pl.ds(row, 48), :],
                            w_sems.at[len(copies)],
                        )
                    )
        for copy in copies:
            copy.start()
        for copy in copies:
            copy.wait()

    whole_w = pltpu.make_async_copy(w_ref, w_out, w_sems.at[32])

    @pl.when(step == 0)
    def _():
        whole_w.start()

    normed, _ = norm_rows(x_ref[...].reshape(ROWS, D).astype(F32))
    nb = (normed * gain_ref[...]).astype(BF16)
    mask = row_mask(counts_ref, step * GROUP, GROUP)
    go = jnp.where(mask, cot_ref[...].reshape(ROWS, D).astype(F32), 0.0).astype(BF16)
    at = pl.ds(pl.multiple_of(step * ROWS, ROWS), ROWS)
    nb_ref[at, :] = nb
    go_ref[at, :] = go

    qk = mm(nb, w_ref[0]).astype(BF16)
    vv = mm(nb, w_ref[1, :, :HD]).astype(BF16)
    ga = mm(go, w_ref[1, :, HD:]).astype(BF16)
    key_id = lax.broadcasted_iota(jnp.int32, (VMAX, 2 * VMAX), 0)
    lane = lax.broadcasted_iota(jnp.int32, (1, 2 * HEAD_DIM), 1)
    first = jnp.where(lane < HEAD_DIM, 1.0, 0.0)
    m0, m1 = first.astype(BF16), (1.0 - first).astype(BF16)
    f0, f1 = (first * factor).astype(BF16), ((1.0 - first) * factor).astype(BF16)
    pair = lambda a, u, w: jnp.concatenate([a * u, a * w], axis=0)
    stack = lambda a: jnp.concatenate([a[:, :VMAX], a[:, VMAX:]], axis=0)
    for b in range(GROUP):
        live = key_id < counts_ref[step * GROUP + b]
        rs = slice(b * VMAX, (b + 1) * VMAX)
        at_b = pl.ds(pl.multiple_of(step * ROWS + b * VMAX, VMAX), VMAX)
        for lo in range(0, HD, 2 * HEAD_DIM):
            hi = lo + 2 * HEAD_DIM
            k = qk[rs, HD + lo : HD + hi]
            v = vv[rs, lo:hi]
            q2 = pair(qk[rs, lo:hi], f0, f1)
            g2 = pair(ga[rs, lo:hi], m0, m1)
            s = jnp.where(live, mm_t(k, q2), -1e30)
            e = jnp.exp(s - jnp.max(s, axis=0, keepdims=True))
            p = e * (1.0 / jnp.sum(e, axis=0, keepdims=True))
            pb = p.astype(BF16)
            dp = mm_t(v, g2)
            ds = (p * (dp - jnp.sum(p * dp, axis=0, keepdims=True))).astype(BF16)
            att_ref[at_b, lo:hi] = tmm(stack(pb), pair(v, m0, m1)).astype(BF16)
            gp_ref[at_b, lo:hi] = tmm(stack(ds), pair(k, f0, f1)).astype(BF16)
            gp_ref[at_b, HD + lo : HD + hi] = mm(ds, q2).astype(BF16)
            gp_ref[at_b, D + lo : D + hi] = mm(pb, g2).astype(BF16)

    def row_copies(i):
        rows = pl.ds(pl.multiple_of(i * ROWS, ROWS), ROWS)
        return (
            pltpu.make_async_copy(att_ref.at[rows, :], att_out.at[rows, :], row_sems.at[0, i]),
            pltpu.make_async_copy(gp_ref.at[rows, :], gp_out.at[rows, :], row_sems.at[1, i]),
        )

    for copy in row_copies(step):
        copy.start()

    @pl.when(step == last)
    def _():
        copies = []
        for i in range(D // 256):
            rr = slice(i * 256, i * 256 + 256)
            gw = tmm(nb_ref[:, rr], gp_ref[...])
            for half, cols, val in (
                (0, slice(0, D), gw[:, :D]),
                (1, slice(0, HD), gw[:, D:]),
                (1, slice(HD, D), tmm(go_ref[:, rr], att_ref[...])),
            ):

                @pl.when(core == half)
                def _():
                    keep_ref[rr, cols] = val

                @pl.when(core != half)
                def _():
                    send_ref[rr, cols] = val.astype(send_ref.dtype)

            copies.append(pltpu.make_async_copy(keep_ref.at[rr, :], keep_out.at[rr, :], dw_sems.at[0, i]))
            copies.append(pltpu.make_async_copy(send_ref.at[rr, :], send_out.at[rr, :], dw_sems.at[1, i]))
            copies[-1].start()
            copies[-2].start()
        whole_w.wait()
        for i in range(BLOCKS // GROUP):
            for copy in row_copies(i):
                copy.wait()
        for copy in copies:
            copy.wait()


def grads_core(at, counts, pieces, tiles, cotan, gain):
    nblock = tiles.shape[0]
    rows = nblock * VMAX
    hbm = pl.BlockSpec(memory_space=pltpu.HBM)
    tile = pl.BlockSpec((GROUP, VMAX, D), lambda i, *_: (i, 0, 0))
    return pl.pallas_call(
        core_kernel,
        grid_spec=pltpu.PrefetchScalarGridSpec(
            num_scalar_prefetch=2,
            grid=(nblock // GROUP,),
            in_specs=[hbm] * 8 + [tile, tile, pl.BlockSpec((1, D), lambda i, *_: (0, 0))],
            out_specs=[hbm] * 3 + [pl.BlockSpec(memory_space=pl.ANY)] * 2,
            scratch_shapes=[
                pltpu.VMEM((2, D, D), BF16),
                pltpu.VMEM((rows, D), BF16),
                pltpu.VMEM((rows, D), BF16),
                pltpu.VMEM((rows, HD), BF16),
                pltpu.VMEM((rows, 3 * HD), BF16),
                pltpu.VMEM((D, D), F32),
                pltpu.VMEM((D, D), BF16),
                pltpu.SemaphoreType.DMA((33,)),
                pltpu.SemaphoreType.DMA((2, nblock // GROUP)),
                pltpu.SemaphoreType.DMA((2, D // 256)),
            ],
        ),
        out_shape=[
            jax.ShapeDtypeStruct((2, D, D), BF16),
            jax.ShapeDtypeStruct((rows, HD), BF16),
            jax.ShapeDtypeStruct((rows, 3 * HD), BF16),
            jax.ShapeDtypeStruct((D, D), F32),
            jax.ShapeDtypeStruct((D, D), BF16),
        ],
        compiler_params=pltpu.CompilerParams(
            dimension_semantics=("arbitrary",), vmem_limit_bytes=CORE_MIB * 1024 * 1024
        ),
        cost_estimate=pl.CostEstimate(flops=20_000_000_000, bytes_accessed=18_000_000, transcendentals=1_200_000),
    )(at, counts, *pieces, tiles, cotan, gain)


def rows_kernel(first, counts_ref, w_ref, att_ref, gp_ref, x_ref, cot_ref, gain_ref, *rest):
    enc_ref, gin_ref = rest[-2:]
    gain = gain_ref[...]
    xf = x_ref[...].reshape(TAIL * VMAX, D).astype(F32)
    normed, inv = norm_rows(xf)
    mask = row_mask(counts_ref, (first + pl.program_id(0)) * TAIL, TAIL)
    enc = xf + mm_t(att_ref[...], w_ref[1, :, HD:])
    enc_ref[...] = jnp.where(mask, enc, 0.0).astype(BF16).reshape(TAIL, VMAX, D)
    gp = gp_ref[...]
    gn = (mm_t(gp[:, :D], w_ref[0]) + mm_t(gp[:, D:], w_ref[1, :, :HD])) * gain
    gl = inv * (
        gn - jnp.mean(gn, axis=-1, keepdims=True) - normed * jnp.mean(gn * normed, axis=-1, keepdims=True)
    )
    gin = cot_ref[...].reshape(TAIL * VMAX, D).astype(F32) + gl
    gin_ref[...] = jnp.where(mask, gin, 0.0).astype(BF16).reshape(TAIL, VMAX, D)


def rows_part(first, count, counts, w, att, gp, tiles, cotan, gain, done):
    tile = pl.BlockSpec((TAIL, VMAX, D), lambda i, *_: (i + first, 0, 0))
    flat = lambda cols: pl.BlockSpec((TAIL * VMAX, cols), lambda i, *_: (i + first, 0))
    return pl.pallas_call(
        functools.partial(rows_kernel, first),
        grid_spec=pltpu.PrefetchScalarGridSpec(
            num_scalar_prefetch=1,
            grid=(count,),
            in_specs=[
                pl.BlockSpec((2, D, D), lambda i, *_: (0, 0, 0), pipeline_mode=pl.Buffered(1)),
                flat(HD),
                flat(3 * HD),
                tile,
                tile,
                pl.BlockSpec((1, D), lambda i, *_: (0, 0)),
            ]
            + [pl.BlockSpec(memory_space=pl.ANY)] * len(done),
            out_specs=[tile, tile],
        ),
        out_shape=[jax.ShapeDtypeStruct(tiles.shape, BF16)] * 2,
        input_output_aliases={7 + i: i for i in range(len(done))},
        compiler_params=pltpu.CompilerParams(
            dimension_semantics=("arbitrary",), vmem_limit_bytes=TAIL_MIB * 1024 * 1024
        ),
        cost_estimate=pl.CostEstimate(
            flops=count * 650_000_000, bytes_accessed=count * 2_500_000, transcendentals=1000
        ),
    )(counts, w, att, gp, tiles, cotan, gain, *done)


def small_call(kernel, at, args, outs):
    smem = [] if at is None else [pl.BlockSpec(memory_space=pltpu.SMEM)]
    vmem = pl.BlockSpec(memory_space=pltpu.VMEM)
    size = sum(a.size * a.dtype.itemsize for a in args)
    return pl.pallas_call(
        kernel,
        in_specs=smem + [vmem] * len(args),
        out_specs=[vmem] * len(outs),
        out_shape=[jax.ShapeDtypeStruct(shape, dtype) for shape, dtype in outs],
        compiler_params=pltpu.CompilerParams(vmem_limit_bytes=12 * 1024 * 1024),
        cost_estimate=pl.CostEstimate(flops=size, bytes_accessed=2 * size, transcendentals=0),
    )(*([] if at is None else [at]), *args)


def cut_kernel(axis, at_ref, own_ref, *refs):
    got, outs = refs[:-4], refs[-4:]
    rows = outs[0].shape[0]
    for k in range(4):
        at = pl.ds(pl.multiple_of(((at_ref[axis] + k) & 3) * rows, rows), rows)
        total = own_ref[at, :]
        for ref in got:
            total = total + ref[at, :].astype(F32)
        outs[k][...] = total.astype(outs[k].dtype)


def cut(at, axis, own, *got):
    rows, n = own.shape[0] // 4, own.shape[1]
    outs = [((rows, n), F32)] + [((rows, n), BF16)] * 3
    return small_call(functools.partial(cut_kernel, axis), at, [own, *got], outs)


def triples_kernel(own_ref, *refs):
    total = own_ref[...]
    for ref in refs[:-1]:
        total = total + ref[...].astype(F32)
    for i in range(16):
        refs[-1][i] = total[3 * i : 3 * i + 3, :]


def finish_kernel(got_ref, qkv_ref, out_ref):
    lo, hi = got_ref[0], got_ref[1]
    for z in range(1, 8):
        lo = lo + got_ref[2 * z]
        hi = hi + got_ref[2 * z + 1]
    qkv_ref[:, :D] = lo
    qkv_ref[:, D:] = hi[:, :HD]
    out_ref[...] = hi[:, HD:]


def scatter_grads(at, keep, send, during):
    own, *out = cut(at, 0, keep, hop_core(send))
    got = [hop_y(v, k + 1) for k, v in enumerate(out)]
    extra = during(own)
    got[0], extra = lax.optimization_barrier((got[0], extra))
    own, *out = cut(at, 1, own, *got)
    parts = [own] + [hop_x(v, k + 1) for k, v in enumerate(out)]
    n = keep.shape[1]
    (v,) = small_call(triples_kernel, None, parts, [((16, 3, n), F32)])
    got = lax.all_to_all(v, "xl", split_axis=0, concat_axis=0, tiled=True)
    return small_call(finish_kernel, None, [got], [((3, n + n // 2), F32), ((3, n // 2), F32)]), extra


def shards(patches, out_cot, vis_count, w_qkv, w_out, ln_gain):
    y, x, z, c = coords()
    pieces = gather_weights(jnp.concatenate([w_qkv, w_out], axis=1))
    at = jnp.stack([y, x, c]).astype(jnp.int32)
    counts, tiles, cotan, gain = vis_count[0], patches[0], out_cot[0], ln_gain[None]
    w, att, gp, keep, send = grads_core(at, counts, pieces, tiles, cotan, gain)

    def during(own):
        late, _ = lax.optimization_barrier((counts, own))
        return rows_part(0, HEAD, late, w, att, gp, tiles, cotan, gain, ())

    (grad_qkv, grad_out), out = scatter_grads(at, keep, send, during)
    enc, gin = rows_part(HEAD, BLOCKS // TAIL - HEAD, counts, w, att, gp, tiles, cotan, gain, out)
    return enc[None], gin[None], grad_qkv, grad_out


def solution(mesh):
    return jax.shard_map(
        shards,
        mesh=mesh,
        in_specs=(
            P("il", "xl", None, None),
            P("il", "xl", None, None),
            P("il", "xl"),
            P(("il", "xl"), None),
            P(("il", "xl"), None),
            P(),
        ),
        out_specs=(
            P("il", "xl", None, None),
            P("il", "xl", None, None),
            P(("il", "xl"), None),
            P(("il", "xl"), None),
        ),
        check_vma=False,
    )
```

```python
import functools

import jax
import jax.numpy as jnp
from jax import lax
from jax.experimental import pallas as pl
from jax.experimental.pallas import tpu as pltpu
from jax.sharding import PartitionSpec as P

HEAD_DIM = 64
HEADS = 6
D = 768
HD = 384
VMAX = 128
BLOCKS = 12
STEPS = (0, 2, 1, 3)
GROUP = 4
ROWS = GROUP * VMAX
TAIL = 2
HEAD = 3
NORM_MIB = 0
CORE_MIB = 48
TAIL_MIB = 60
BF16 = jnp.bfloat16
F32 = jnp.float32


def hop_x(v, k):
    return lax.ppermute(v, "il", [(i, (i // 4) * 4 + (i + k) % 4) for i in range(16)])


def hop_y(v, k):
    return lax.ppermute(v, "il", [(i, (i + 4 * k) % 16) for i in range(16)])


def hop_z(v, k):
    return lax.ppermute(v, "xl", [(i, (i + 2 * k) % 16) for i in range(16)])


def hop_core(v):
    return lax.ppermute(v, "xl", [(i, i ^ 1) for i in range(16)])


def coords():
    il = lax.axis_index("il")
    xl = lax.axis_index("xl")
    return il // 4, il % 4, xl // 2, xl % 2


def gather4(v, hop):
    return [v, hop(v, 2), hop(v, -1), hop(v, 1)]


def gather_weights(w):
    y, x, z, c = coords()
    n = w.shape[1] // 2
    mine = lax.dynamic_slice(w, (0, c * n), (3, n))
    other = lax.dynamic_slice(w, (0, (1 - c) * n), (3, n))
    block = jnp.concatenate([mine, hop_core(other), jnp.zeros((2, n), w.dtype)], axis=0)
    block = jnp.concatenate([block, lax.ppermute(block, "xl", [(i, i ^ 2) for i in range(16)])], axis=0)
    stack = jnp.concatenate([block, hop_z(block, 4), hop_z(block, 2), hop_z(block, -2)], axis=0)
    r = jnp.arange(48)[:, None]
    s = jnp.arange(64)[None, :]
    slot = s // 16
    j = s % 8
    origin = (z + jnp.where(slot == 1, 4, jnp.where(slot == 2, 6, jnp.where(slot == 3, 2, 0)))) % 8
    row = (origin ^ ((s // 8) % 2)) * 6 + (c ^ (j // 3)) * 3 + j % 3
    order = ((row == r) & (j < 6)).astype(w.dtype)
    v = jnp.dot(order, stack, preferred_element_type=F32).astype(w.dtype)
    v = jnp.concatenate(gather4(v, hop_x), axis=0)
    mine = gather4(v, hop_y)
    return mine + [hop_core(u) for u in mine]


def mm(a, b):
    return jnp.dot(a, b, preferred_element_type=F32)


def mm_t(a, b):
    return lax.dot_general(a, b, (((1,), (1,)), ((), ())), preferred_element_type=F32)


def tmm(a, b):
    return lax.dot_general(a, b, (((0,), (0,)), ((), ())), preferred_element_type=F32)


def norm_rows(xf):
    centred = xf - jnp.mean(xf, axis=-1, keepdims=True)
    inv = lax.rsqrt(jnp.mean(centred * centred, axis=-1, keepdims=True) + 1e-6)
    return centred * inv, inv


def row_mask(counts_ref, first, group):
    row_id = lax.broadcasted_iota(jnp.int32, (VMAX, D), 0)
    return jnp.concatenate([row_id < counts_ref[first + b] for b in range(group)], axis=0)


def core_kernel(*refs):
    at_ref, counts_ref = refs[:2]
    pieces = refs[2:10]
    x_ref, cot_ref, gain_ref = refs[10:13]
    w_out, att_out, gp_out, keep_out, send_out = refs[13:18]
    w_ref, nb_ref, go_ref, att_ref, gp_ref, keep_ref, send_ref, w_sems, row_sems, dw_sems = refs[18:]
    step = pl.program_id(0)
    last = pl.num_programs(0) - 1
    factor = HEAD_DIM**-0.5
    core = at_ref[2]

    @pl.when(step == 0)
    def _():
        y, x = at_ref[0], at_ref[1]
        copies = []
        for rel in range(2):
            half = core ^ rel
            for ky in range(4):
                for kx in range(4):
                    row = pl.multiple_of(((y + STEPS[ky]) & 3) * 192 + ((x + STEPS[kx]) & 3) * 48, 16)
                    copies.append(
                        pltpu.make_async_copy(
                            pieces[rel * 4 + ky].at[pl.ds(kx * 48, 48), :],
                            w_ref.at[half, pl.ds(row, 48), :],
                            w_sems.at[len(copies)],
                        )
                    )
        for copy in copies:
            copy.start()
        for copy in copies:
            copy.wait()

    whole_w = pltpu.make_async_copy(w_ref, w_out, w_sems.at[32])

    @pl.when(step == 0)
    def _():
        whole_w.start()

    normed, _ = norm_rows(x_ref[...].reshape(ROWS, D).astype(F32))
    nb = (normed * gain_ref[...]).astype(BF16)
    mask = row_mask(counts_ref, step * GROUP, GROUP)
    go = jnp.where(mask, cot_ref[...].reshape(ROWS, D).astype(F32), 0.0).astype(BF16)
    at = pl.ds(pl.multiple_of(step * ROWS, ROWS), ROWS)
    nb_ref[at, :] = nb
    go_ref[at, :] = go

    qk = mm(nb, w_ref[0]).astype(BF16)
    vv = mm(nb, w_ref[1, :, :HD]).astype(BF16)
    ga = mm(go, w_ref[1, :, HD:]).astype(BF16)
    key_id = lax.broadcasted_iota(jnp.int32, (VMAX, 2 * VMAX), 0)
    lane = lax.broadcasted_iota(jnp.int32, (1, 2 * HEAD_DIM), 1)
    first = jnp.where(lane < HEAD_DIM, 1.0, 0.0)
    m0, m1 = first.astype(BF16), (1.0 - first).astype(BF16)
    f0, f1 = (first * factor).astype(BF16), ((1.0 - first) * factor).astype(BF16)
    pair = lambda a, u, w: jnp.concatenate([a * u, a * w], axis=0)
    stack = lambda a: jnp.concatenate([a[:, :VMAX], a[:, VMAX:]], axis=0)
    for b in range(GROUP):
        live = key_id < counts_ref[step * GROUP + b]
        rs = slice(b * VMAX, (b + 1) * VMAX)
        at_b = pl.ds(pl.multiple_of(step * ROWS + b * VMAX, VMAX), VMAX)
        for lo in range(0, HD, 2 * HEAD_DIM):
            hi = lo + 2 * HEAD_DIM
            k = qk[rs, HD + lo : HD + hi]
            v = vv[rs, lo:hi]
            q2 = pair(qk[rs, lo:hi], f0, f1)
            g2 = pair(ga[rs, lo:hi], m0, m1)
            s = jnp.where(live, mm_t(k, q2), -1e30)
            e = jnp.exp(s - jnp.max(s, axis=0, keepdims=True))
            p = e * (1.0 / jnp.sum(e, axis=0, keepdims=True))
            pb = p.astype(BF16)
            dp = mm_t(v, g2)
            ds = (p * (dp - jnp.sum(p * dp, axis=0, keepdims=True))).astype(BF16)
            att_ref[at_b, lo:hi] = tmm(stack(pb), pair(v, m0, m1)).astype(BF16)
            gp_ref[at_b, lo:hi] = tmm(stack(ds), pair(k, f0, f1)).astype(BF16)
            gp_ref[at_b, HD + lo : HD + hi] = mm(ds, q2).astype(BF16)
            gp_ref[at_b, D + lo : D + hi] = mm(pb, g2).astype(BF16)

    def row_copies(i):
        rows = pl.ds(pl.multiple_of(i * ROWS, ROWS), ROWS)
        return (
            pltpu.make_async_copy(att_ref.at[rows, :], att_out.at[rows, :], row_sems.at[0, i]),
            pltpu.make_async_copy(gp_ref.at[rows, :], gp_out.at[rows, :], row_sems.at[1, i]),
        )

    for copy in row_copies(step):
        copy.start()

    @pl.when(step == last)
    def _():
        copies = []
        for i in range(D // 256):
            rr = slice(i * 256, i * 256 + 256)
            gw = tmm(nb_ref[:, rr], gp_ref[...])
            for half, cols, val in (
                (0, slice(0, D), gw[:, :D]),
                (1, slice(0, HD), gw[:, D:]),
                (1, slice(HD, D), tmm(go_ref[:, rr], att_ref[...])),
            ):

                @pl.when(core == half)
                def _():
                    keep_ref[rr, cols] = val

                @pl.when(core != half)
                def _():
                    send_ref[rr, cols] = val.astype(send_ref.dtype)

            copies.append(pltpu.make_async_copy(keep_ref.at[rr, :], keep_out.at[rr, :], dw_sems.at[0, i]))
            copies.append(pltpu.make_async_copy(send_ref.at[rr, :], send_out.at[rr, :], dw_sems.at[1, i]))
            copies[-1].start()
            copies[-2].start()
        whole_w.wait()
        for i in range(BLOCKS // GROUP):
            for copy in row_copies(i):
                copy.wait()
        for copy in copies:
            copy.wait()


def grads_core(at, counts, pieces, tiles, cotan, gain):
    nblock = tiles.shape[0]
    rows = nblock * VMAX
    hbm = pl.BlockSpec(memory_space=pltpu.HBM)
    tile = pl.BlockSpec((GROUP, VMAX, D), lambda i, *_: (i, 0, 0))
    return pl.pallas_call(
        core_kernel,
        grid_spec=pltpu.PrefetchScalarGridSpec(
            num_scalar_prefetch=2,
            grid=(nblock // GROUP,),
            in_specs=[hbm] * 8 + [tile, tile, pl.BlockSpec((1, D), lambda i, *_: (0, 0))],
            out_specs=[hbm] * 3 + [pl.BlockSpec(memory_space=pl.ANY)] * 2,
            scratch_shapes=[
                pltpu.VMEM((2, D, D), BF16),
                pltpu.VMEM((rows, D), BF16),
                pltpu.VMEM((rows, D), BF16),
                pltpu.VMEM((rows, HD), BF16),
                pltpu.VMEM((rows, 3 * HD), BF16),
                pltpu.VMEM((D, D), F32),
                pltpu.VMEM((D, D), BF16),
                pltpu.SemaphoreType.DMA((33,)),
                pltpu.SemaphoreType.DMA((2, nblock // GROUP)),
                pltpu.SemaphoreType.DMA((2, D // 256)),
            ],
        ),
        out_shape=[
            pltpu.HBM((2, D, D), BF16),
            pltpu.HBM((rows, HD), BF16),
            pltpu.HBM((rows, 3 * HD), BF16),
            jax.ShapeDtypeStruct((D, D), F32),
            jax.ShapeDtypeStruct((D, D), BF16),
        ],
        compiler_params=pltpu.CompilerParams(
            dimension_semantics=("arbitrary",), vmem_limit_bytes=CORE_MIB * 1024 * 1024
        ),
        cost_estimate=pl.CostEstimate(flops=20_000_000_000, bytes_accessed=18_000_000, transcendentals=1_200_000),
    )(at, counts, *pieces, tiles, cotan, gain)


def rows_kernel(first, counts_ref, w_ref, att_ref, gp_ref, x_ref, cot_ref, gain_ref, *rest):
    enc_ref, gin_ref = rest[-2:]
    gain = gain_ref[...]
    xf = x_ref[...].reshape(TAIL * VMAX, D).astype(F32)
    normed, inv = norm_rows(xf)
    mask = row_mask(counts_ref, (first + pl.program_id(0)) * TAIL, TAIL)
    enc = xf + mm_t(att_ref[...], w_ref[1, :, HD:])
    enc_ref[...] = jnp.where(mask, enc, 0.0).astype(BF16).reshape(TAIL, VMAX, D)
    gp = gp_ref[...]
    gn = (mm_t(gp[:, :D], w_ref[0]) + mm_t(gp[:, D:], w_ref[1, :, :HD])) * gain
    gl = inv * (
        gn - jnp.mean(gn, axis=-1, keepdims=True) - normed * jnp.mean(gn * normed, axis=-1, keepdims=True)
    )
    gin = cot_ref[...].reshape(TAIL * VMAX, D).astype(F32) + gl
    gin_ref[...] = jnp.where(mask, gin, 0.0).astype(BF16).reshape(TAIL, VMAX, D)


def rows_part(first, count, counts, w, att, gp, tiles, cotan, gain, done):
    tile = pl.BlockSpec((TAIL, VMAX, D), lambda i, *_: (i + first, 0, 0))
    flat = lambda cols: pl.BlockSpec((TAIL * VMAX, cols), lambda i, *_: (i + first, 0))
    return pl.pallas_call(
        functools.partial(rows_kernel, first),
        grid_spec=pltpu.PrefetchScalarGridSpec(
            num_scalar_prefetch=1,
            grid=(count,),
            in_specs=[
                pl.BlockSpec((2, D, D), lambda i, *_: (0, 0, 0), pipeline_mode=pl.Buffered(1)),
                flat(HD),
                flat(3 * HD),
                tile,
                tile,
                pl.BlockSpec((1, D), lambda i, *_: (0, 0)),
            ]
            + [pl.BlockSpec(memory_space=pl.ANY)] * len(done),
            out_specs=[tile, tile],
        ),
        out_shape=[jax.ShapeDtypeStruct(tiles.shape, BF16)] * 2,
        input_output_aliases={7 + i: i for i in range(len(done))},
        compiler_params=pltpu.CompilerParams(
            dimension_semantics=("arbitrary",), vmem_limit_bytes=TAIL_MIB * 1024 * 1024
        ),
        cost_estimate=pl.CostEstimate(
            flops=count * 650_000_000, bytes_accessed=count * 2_500_000, transcendentals=1000
        ),
    )(counts, w, att, gp, tiles, cotan, gain, *done)


def small_call(kernel, at, args, outs):
    smem = [] if at is None else [pl.BlockSpec(memory_space=pltpu.SMEM)]
    vmem = pl.BlockSpec(memory_space=pltpu.VMEM)
    size = sum(a.size * a.dtype.itemsize for a in args)
    return pl.pallas_call(
        kernel,
        in_specs=smem + [vmem] * len(args),
        out_specs=[vmem] * len(outs),
        out_shape=[jax.ShapeDtypeStruct(shape, dtype) for shape, dtype in outs],
        compiler_params=pltpu.CompilerParams(vmem_limit_bytes=12 * 1024 * 1024),
        cost_estimate=pl.CostEstimate(flops=size, bytes_accessed=2 * size, transcendentals=0),
    )(*([] if at is None else [at]), *args)


def cut_kernel(axis, at_ref, own_ref, *refs):
    got, outs = refs[:-4], refs[-4:]
    rows = outs[0].shape[0]
    for k in range(4):
        at = pl.ds(pl.multiple_of(((at_ref[axis] + k) & 3) * rows, rows), rows)
        total = own_ref[at, :]
        for ref in got:
            total = total + ref[at, :].astype(F32)
        outs[k][...] = total.astype(outs[k].dtype)


def cut(at, axis, own, *got):
    rows, n = own.shape[0] // 4, own.shape[1]
    outs = [((rows, n), F32)] + [((rows, n), BF16)] * 3
    return small_call(functools.partial(cut_kernel, axis), at, [own, *got], outs)


def triples_kernel(own_ref, *refs):
    total = own_ref[...]
    for ref in refs[:-1]:
        total = total + ref[...].astype(F32)
    for i in range(16):
        refs[-1][i] = total[3 * i : 3 * i + 3, :]


def finish_kernel(got_ref, qkv_ref, out_ref):
    lo, hi = got_ref[0], got_ref[1]
    for z in range(1, 8):
        lo = lo + got_ref[2 * z]
        hi = hi + got_ref[2 * z + 1]
    qkv_ref[:, :D] = lo
    qkv_ref[:, D:] = hi[:, :HD]
    out_ref[...] = hi[:, HD:]


def scatter_grads(at, keep, send, during):
    own, *out = cut(at, 0, keep, hop_core(send))
    got = [hop_y(out[k - 1], k) for k in (2, 1, 3)]
    extra = during(own)
    got[0], extra = lax.optimization_barrier((got[0], extra))
    own, *out = cut(at, 1, own, *got)
    parts = [own] + [hop_x(out[k - 1], k) for k in (2, 1, 3)]
    n = keep.shape[1]
    (v,) = small_call(triples_kernel, None, parts, [((16, 3, n), F32)])
    got = lax.all_to_all(v, "xl", split_axis=0, concat_axis=0, tiled=True)
    return small_call(finish_kernel, None, [got], [((3, n + n // 2), F32), ((3, n // 2), F32)]), extra


def shards(patches, out_cot, vis_count, w_qkv, w_out, ln_gain):
    y, x, z, c = coords()
    pieces = gather_weights(jnp.concatenate([w_qkv, w_out], axis=1))
    at = jnp.stack([y, x, c]).astype(jnp.int32)
    counts, tiles, cotan, gain = vis_count[0], patches[0], out_cot[0], ln_gain[None]
    w, att, gp, keep, send = grads_core(at, counts, pieces, tiles, cotan, gain)

    def during(own):
        late, _ = lax.optimization_barrier((counts, own))
        return rows_part(0, HEAD, late, w, att, gp, tiles, cotan, gain, ())

    (grad_qkv, grad_out), out = scatter_grads(at, keep, send, during)
    enc, gin = rows_part(HEAD, BLOCKS // TAIL - HEAD, counts, w, att, gp, tiles, cotan, gain, out)
    return enc[None], gin[None], grad_qkv, grad_out


def solution(mesh):
    return jax.shard_map(
        shards,
        mesh=mesh,
        in_specs=(
            P("il", "xl", None, None),
            P("il", "xl", None, None),
            P("il", "xl"),
            P(("il", "xl"), None),
            P(("il", "xl"), None),
            P(),
        ),
        out_specs=(
            P("il", "xl", None, None),
            P("il", "xl", None, None),
            P(("il", "xl"), None),
            P(("il", "xl"), None),
        ),
        check_vma=False,
    )
```

```python
import functools

import jax
import jax.numpy as jnp
from jax import lax
from jax.experimental import pallas as pl
from jax.experimental.pallas import tpu as pltpu
from jax.sharding import PartitionSpec as P

HEAD_DIM = 64
HEADS = 6
D = 768
HD = 384
VMAX = 128
BLOCKS = 12
STEPS = (0, 2, 1, 3)
GROUP = 4
ROWS = GROUP * VMAX
TAIL = 2
HEAD = 3
NORM_MIB = 0
CORE_MIB = 48
TAIL_MIB = 60
BF16 = jnp.bfloat16
F32 = jnp.float32


def hop_x(v, k):
    return lax.ppermute(v, "il", [(i, (i // 4) * 4 + (i + k) % 4) for i in range(16)])


def hop_y(v, k):
    return lax.ppermute(v, "il", [(i, (i + 4 * k) % 16) for i in range(16)])


def hop_z(v, k):
    return lax.ppermute(v, "xl", [(i, (i + 2 * k) % 16) for i in range(16)])


def hop_core(v):
    return lax.ppermute(v, "xl", [(i, i ^ 1) for i in range(16)])


def coords():
    il = lax.axis_index("il")
    xl = lax.axis_index("xl")
    return il // 4, il % 4, xl // 2, xl % 2


def gather4(v, hop):
    return [v, hop(v, 2), hop(v, -1), hop(v, 1)]


def gather_weights(w_qkv, w_out):
    y, x, z, c = coords()
    n = D
    left = w_qkv[:, :n]
    right = jnp.concatenate([w_qkv[:, n:], w_out], axis=1)
    mine = jnp.where(c == 0, left, right)
    other = jnp.where(c == 0, right, left)
    block = jnp.concatenate([mine, hop_core(other), jnp.zeros((2, n), BF16)], axis=0)
    block = jnp.concatenate([block, lax.ppermute(block, "xl", [(i, i ^ 2) for i in range(16)])], axis=0)
    stack = jnp.concatenate([block, hop_z(block, 4), hop_z(block, 2), hop_z(block, -2)], axis=0)
    r = jnp.arange(48)[:, None]
    s = jnp.arange(64)[None, :]
    slot = s // 16
    j = s % 8
    origin = (z + jnp.where(slot == 1, 4, jnp.where(slot == 2, 6, jnp.where(slot == 3, 2, 0)))) % 8
    row = (origin ^ ((s // 8) % 2)) * 6 + (c ^ (j // 3)) * 3 + j % 3
    order = ((row == r) & (j < 6)).astype(BF16)
    v = jnp.dot(order, stack, preferred_element_type=F32).astype(BF16)
    v = jnp.concatenate(gather4(v, hop_x), axis=0)
    mine = gather4(v, hop_y)
    return mine + [hop_core(u) for u in mine]


def mm(a, b):
    return jnp.dot(a, b, preferred_element_type=F32)


def mm_t(a, b):
    return lax.dot_general(a, b, (((1,), (1,)), ((), ())), preferred_element_type=F32)


def tmm(a, b):
    return lax.dot_general(a, b, (((0,), (0,)), ((), ())), preferred_element_type=F32)


def norm_rows(xf):
    centred = xf - jnp.mean(xf, axis=-1, keepdims=True)
    inv = lax.rsqrt(jnp.mean(centred * centred, axis=-1, keepdims=True) + 1e-6)
    return centred * inv, inv


def row_mask(at_ref, first, group):
    row_id = lax.broadcasted_iota(jnp.int32, (VMAX, D), 0)
    return jnp.concatenate([row_id < at_ref[3 + first + b] for b in range(group)], axis=0)


def core_kernel(*refs):
    at_ref = refs[0]
    pieces = refs[1:9]
    x_ref, cot_ref, gain_ref = refs[9:12]
    w_out, att_out, gp_out, keep_out, send_out = refs[12:17]
    w_ref, nb_ref, go_ref, att_ref, gp_ref, keep_ref, send_ref, w_sems, row_sems, dw_sems = refs[17:]
    step = pl.program_id(0)
    last = pl.num_programs(0) - 1
    factor = HEAD_DIM**-0.5
    core = at_ref[2]

    def weight_copies():
        y, x = at_ref[0], at_ref[1]
        copies = []
        for rel in range(2):
            half = core ^ rel
            for ky in range(4):
                for kx in range(4):
                    row = pl.multiple_of(((y + STEPS[ky]) & 3) * 192 + ((x + STEPS[kx]) & 3) * 48, 16)
                    copies.append(
                        pltpu.make_async_copy(
                            pieces[rel * 4 + ky].at[pl.ds(kx * 48, 48), :],
                            w_ref.at[half, pl.ds(row, 48), :],
                            w_sems.at[len(copies)],
                        )
                    )
        return copies

    @pl.when(step == 0)
    def _():
        for copy in weight_copies():
            copy.start()

    whole_w = pltpu.make_async_copy(w_ref, w_out, w_sems.at[32])

    normed, _ = norm_rows(x_ref[...].reshape(ROWS, D).astype(F32))
    nb = (normed * gain_ref[...]).astype(BF16)
    mask = row_mask(at_ref, step * GROUP, GROUP)
    go = jnp.where(mask, cot_ref[...].reshape(ROWS, D).astype(F32), 0.0).astype(BF16)
    at = pl.ds(pl.multiple_of(step * ROWS, ROWS), ROWS)
    nb_ref[at, :] = nb
    go_ref[at, :] = go

    @pl.when(step == 0)
    def _():
        for copy in weight_copies():
            copy.wait()
        whole_w.start()

    qk = mm(nb, w_ref[0]).astype(BF16)
    vv = mm(nb, w_ref[1, :, :HD]).astype(BF16)
    ga = mm(go, w_ref[1, :, HD:]).astype(BF16)
    key_id = lax.broadcasted_iota(jnp.int32, (VMAX, 2 * VMAX), 0)
    lane = lax.broadcasted_iota(jnp.int32, (1, 2 * HEAD_DIM), 1)
    first = jnp.where(lane < HEAD_DIM, 1.0, 0.0)
    m0, m1 = first.astype(BF16), (1.0 - first).astype(BF16)
    f0, f1 = (first * factor).astype(BF16), ((1.0 - first) * factor).astype(BF16)
    pair = lambda a, u, w: jnp.concatenate([a * u, a * w], axis=0)
    stack = lambda a: jnp.concatenate([a[:, :VMAX], a[:, VMAX:]], axis=0)
    for b in range(GROUP):
        live = key_id < at_ref[3 + step * GROUP + b]
        rs = slice(b * VMAX, (b + 1) * VMAX)
        at_b = pl.ds(pl.multiple_of(step * ROWS + b * VMAX, VMAX), VMAX)
        for lo in range(0, HD, 2 * HEAD_DIM):
            hi = lo + 2 * HEAD_DIM
            k = qk[rs, HD + lo : HD + hi]
            v = vv[rs, lo:hi]
            q2 = pair(qk[rs, lo:hi], f0, f1)
            g2 = pair(ga[rs, lo:hi], m0, m1)
            s = jnp.where(live, mm_t(k, q2), -1e30)
            e = jnp.exp(s - jnp.max(s, axis=0, keepdims=True))
            p = e * (1.0 / jnp.sum(e, axis=0, keepdims=True))
            pb = p.astype(BF16)
            dp = mm_t(v, g2)
            ds = (p * (dp - jnp.sum(p * dp, axis=0, keepdims=True))).astype(BF16)
            att_ref[at_b, lo:hi] = tmm(stack(pb), pair(v, m0, m1)).astype(BF16)
            gp_ref[at_b, lo:hi] = tmm(stack(ds), pair(k, f0, f1)).astype(BF16)
            gp_ref[at_b, HD + lo : HD + hi] = mm(ds, q2).astype(BF16)
            gp_ref[at_b, D + lo : D + hi] = mm(pb, g2).astype(BF16)

    def row_copies(i):
        rows = pl.ds(pl.multiple_of(i * ROWS, ROWS), ROWS)
        return (
            pltpu.make_async_copy(att_ref.at[rows, :], att_out.at[rows, :], row_sems.at[0, i]),
            pltpu.make_async_copy(gp_ref.at[rows, :], gp_out.at[rows, :], row_sems.at[1, i]),
        )

    for copy in row_copies(step):
        copy.start()

    @pl.when(step == last)
    def _():
        copies = []
        for i in range(D // 256):
            rr = slice(i * 256, i * 256 + 256)
            gw = tmm(nb_ref[:, rr], gp_ref[...])
            for half, cols, val in (
                (0, slice(0, D), gw[:, :D]),
                (1, slice(0, HD), gw[:, D:]),
                (1, slice(HD, D), tmm(go_ref[:, rr], att_ref[...])),
            ):

                @pl.when(core == half)
                def _():
                    keep_ref[rr, cols] = val

                @pl.when(core != half)
                def _():
                    send_ref[rr, cols] = val.astype(send_ref.dtype)

            copies.append(pltpu.make_async_copy(keep_ref.at[rr, :], keep_out.at[rr, :], dw_sems.at[0, i]))
            copies.append(pltpu.make_async_copy(send_ref.at[rr, :], send_out.at[rr, :], dw_sems.at[1, i]))
            copies[-1].start()
            copies[-2].start()
        whole_w.wait()
        for i in range(BLOCKS // GROUP):
            for copy in row_copies(i):
                copy.wait()
        for copy in copies:
            copy.wait()


def grads_core(at, pieces, tiles, cotan, gain):
    nblock = tiles.shape[0]
    rows = nblock * VMAX
    hbm = pl.BlockSpec(memory_space=pltpu.HBM)
    tile = pl.BlockSpec((GROUP, VMAX, D), lambda i, *_: (i, 0, 0))
    return pl.pallas_call(
        core_kernel,
        grid_spec=pltpu.PrefetchScalarGridSpec(
            num_scalar_prefetch=1,
            grid=(nblock // GROUP,),
            in_specs=[hbm] * 8 + [tile, tile, pl.BlockSpec((1, D), lambda i, *_: (0, 0))],
            out_specs=[hbm] * 3 + [pl.BlockSpec(memory_space=pl.ANY)] * 2,
            scratch_shapes=[
                pltpu.VMEM((2, D, D), BF16),
                pltpu.VMEM((rows, D), BF16),
                pltpu.VMEM((rows, D), BF16),
                pltpu.VMEM((rows, HD), BF16),
                pltpu.VMEM((rows, 3 * HD), BF16),
                pltpu.VMEM((D, D), F32),
                pltpu.VMEM((D, D), BF16),
                pltpu.SemaphoreType.DMA((33,)),
                pltpu.SemaphoreType.DMA((2, nblock // GROUP)),
                pltpu.SemaphoreType.DMA((2, D // 256)),
            ],
        ),
        out_shape=[
            pltpu.HBM((2, D, D), BF16),
            pltpu.HBM((rows, HD), BF16),
            pltpu.HBM((rows, 3 * HD), BF16),
            jax.ShapeDtypeStruct((D, D), F32),
            jax.ShapeDtypeStruct((D, D), BF16),
        ],
        compiler_params=pltpu.CompilerParams(
            dimension_semantics=("arbitrary",), vmem_limit_bytes=CORE_MIB * 1024 * 1024
        ),
        cost_estimate=pl.CostEstimate(flops=20_000_000_000, bytes_accessed=18_000_000, transcendentals=1_200_000),
    )(at, *pieces, tiles, cotan, gain)


def rows_kernel(first, at_ref, w_ref, att_ref, gp_ref, x_ref, cot_ref, gain_ref, *rest):
    enc_ref, gin_ref = rest[-2:]
    gain = gain_ref[...]
    xf = x_ref[...].reshape(TAIL * VMAX, D).astype(F32)
    normed, inv = norm_rows(xf)
    mask = row_mask(at_ref, (first + pl.program_id(0)) * TAIL, TAIL)
    enc = xf + mm_t(att_ref[...], w_ref[1, :, HD:])
    enc_ref[...] = jnp.where(mask, enc, 0.0).astype(BF16).reshape(TAIL, VMAX, D)
    gp = gp_ref[...]
    gn = (mm_t(gp[:, :D], w_ref[0]) + mm_t(gp[:, D:], w_ref[1, :, :HD])) * gain
    gl = inv * (
        gn - jnp.mean(gn, axis=-1, keepdims=True) - normed * jnp.mean(gn * normed, axis=-1, keepdims=True)
    )
    gin = cot_ref[...].reshape(TAIL * VMAX, D).astype(F32) + gl
    gin_ref[...] = jnp.where(mask, gin, 0.0).astype(BF16).reshape(TAIL, VMAX, D)


def rows_part(first, count, at, w, att, gp, tiles, cotan, gain, done):
    tile = pl.BlockSpec((TAIL, VMAX, D), lambda i, *_: (i + first, 0, 0))
    flat = lambda cols: pl.BlockSpec((TAIL * VMAX, cols), lambda i, *_: (i + first, 0))
    return pl.pallas_call(
        functools.partial(rows_kernel, first),
        grid_spec=pltpu.PrefetchScalarGridSpec(
            num_scalar_prefetch=1,
            grid=(count,),
            in_specs=[
                pl.BlockSpec((2, D, D), lambda i, *_: (0, 0, 0), pipeline_mode=pl.Buffered(1)),
                flat(HD),
                flat(3 * HD),
                tile,
                tile,
                pl.BlockSpec((1, D), lambda i, *_: (0, 0)),
            ]
            + [pl.BlockSpec(memory_space=pl.ANY)] * len(done),
            out_specs=[tile, tile],
        ),
        out_shape=[jax.ShapeDtypeStruct(tiles.shape, BF16)] * 2,
        input_output_aliases={7 + i: i for i in range(len(done))},
        compiler_params=pltpu.CompilerParams(
            dimension_semantics=("arbitrary",), vmem_limit_bytes=TAIL_MIB * 1024 * 1024
        ),
        cost_estimate=pl.CostEstimate(
            flops=count * 650_000_000, bytes_accessed=count * 2_500_000, transcendentals=1000
        ),
    )(at, w, att, gp, tiles, cotan, gain, *done)


def small_call(kernel, at, args, outs):
    smem = [] if at is None else [pl.BlockSpec(memory_space=pltpu.SMEM)]
    vmem = pl.BlockSpec(memory_space=pltpu.VMEM)
    size = sum(a.size * a.dtype.itemsize for a in args)
    return pl.pallas_call(
        kernel,
        in_specs=smem + [vmem] * len(args),
        out_specs=[vmem] * len(outs),
        out_shape=[jax.ShapeDtypeStruct(shape, dtype) for shape, dtype in outs],
        compiler_params=pltpu.CompilerParams(vmem_limit_bytes=12 * 1024 * 1024),
        cost_estimate=pl.CostEstimate(flops=size, bytes_accessed=2 * size, transcendentals=0),
    )(*([] if at is None else [at]), *args)


def cut_kernel(axis, at_ref, own_ref, *refs):
    got, outs = refs[:-4], refs[-4:]
    rows = outs[0].shape[0]
    for k in range(4):
        at = pl.ds(pl.multiple_of(((at_ref[axis] + k) & 3) * rows, rows), rows)
        total = own_ref[at, :]
        for ref in got:
            total = total + ref[at, :].astype(F32)
        outs[k][...] = total.astype(outs[k].dtype)


def cut(at, axis, own, *got):
    rows, n = own.shape[0] // 4, own.shape[1]
    outs = [((rows, n), F32)] + [((rows, n), BF16)] * 3
    return small_call(functools.partial(cut_kernel, axis), at, [own, *got], outs)


def triples_kernel(own_ref, *refs):
    total = own_ref[...]
    for ref in refs[:-1]:
        total = total + ref[...].astype(F32)
    for i in range(16):
        refs[-1][i] = total[3 * i : 3 * i + 3, :]


def finish_kernel(got_ref, qkv_ref, out_ref):
    lo, hi = got_ref[0], got_ref[1]
    for z in range(1, 8):
        lo = lo + got_ref[2 * z]
        hi = hi + got_ref[2 * z + 1]
    qkv_ref[:, :D] = lo
    qkv_ref[:, D:] = hi[:, :HD]
    out_ref[...] = hi[:, HD:]


def scatter_grads(at, keep, send, during):
    own, *out = cut(at, 0, keep, hop_core(send))
    got = [hop_y(out[k - 1], k) for k in (2, 1, 3)]
    extra = during(own)
    got[0], extra = lax.optimization_barrier((got[0], extra))
    own, *out = cut(at, 1, own, *got)
    parts = [own] + [hop_x(out[k - 1], k) for k in (2, 1, 3)]
    n = keep.shape[1]
    (v,) = small_call(triples_kernel, None, parts, [((16, 3, n), F32)])
    got = lax.all_to_all(v, "xl", split_axis=0, concat_axis=0, tiled=True)
    return small_call(finish_kernel, None, [got], [((3, n + n // 2), F32), ((3, n // 2), F32)]), extra


def shards(patches, out_cot, vis_count, w_qkv, w_out, ln_gain):
    y, x, z, c = coords()
    pieces = gather_weights(w_qkv, w_out)
    at = jnp.concatenate([jnp.stack([y, x, c]).astype(jnp.int32), vis_count[0]])
    tiles, cotan, gain = patches[0], out_cot[0], ln_gain[None]
    w, att, gp, keep, send = grads_core(at, pieces, tiles, cotan, gain)

    def during(own):
        late, _ = lax.optimization_barrier((at, own))
        return rows_part(0, HEAD, late, w, att, gp, tiles, cotan, gain, ())

    (grad_qkv, grad_out), out = scatter_grads(at, keep, send, during)
    enc, gin = rows_part(HEAD, BLOCKS // TAIL - HEAD, at, w, att, gp, tiles, cotan, gain, out)
    return enc[None], gin[None], grad_qkv, grad_out


def solution(mesh):
    return jax.shard_map(
        shards,
        mesh=mesh,
        in_specs=(
            P("il", "xl", None, None),
            P("il", "xl", None, None),
            P("il", "xl"),
            P(("il", "xl"), None),
            P(("il", "xl"), None),
            P(),
        ),
        out_specs=(
            P("il", "xl", None, None),
            P("il", "xl", None, None),
            P(("il", "xl"), None),
            P(("il", "xl"), None),
        ),
        check_vma=False,
    )
```

```python
import functools

import jax
import jax.numpy as jnp
from jax import lax
from jax.experimental import pallas as pl
from jax.experimental.pallas import tpu as pltpu
from jax.sharding import PartitionSpec as P

HEAD_DIM = 64
HEADS = 6
D = 768
HD = 384
VMAX = 128
BLOCKS = 12
STEPS = (0, 2, 1, 3)
GROUP = 4
ROWS = GROUP * VMAX
TAIL = 2
HEAD = 3
NORM_MIB = 0
CORE_MIB = 48
TAIL_MIB = 60
BF16 = jnp.bfloat16
F32 = jnp.float32


def hop_x(v, k):
    return lax.ppermute(v, "il", [(i, (i // 4) * 4 + (i + k) % 4) for i in range(16)])


def hop_y(v, k):
    return lax.ppermute(v, "il", [(i, (i + 4 * k) % 16) for i in range(16)])


def hop_z(v, k):
    return lax.ppermute(v, "xl", [(i, (i + 2 * k) % 16) for i in range(16)])


def hop_core(v):
    return lax.ppermute(v, "xl", [(i, i ^ 1) for i in range(16)])


def coords():
    il = lax.axis_index("il")
    xl = lax.axis_index("xl")
    return il // 4, il % 4, xl // 2, xl % 2


def gather4(v, hop):
    return [v, hop(v, 2), hop(v, -1), hop(v, 1)]


def gather_weights(w_qkv, w_out):
    y, x, z, c = coords()
    n = D
    left = w_qkv[:, :n]
    right = jnp.concatenate([w_qkv[:, n:], w_out], axis=1)
    mine = jnp.where(c == 0, left, right)
    other = jnp.where(c == 0, right, left)
    block = jnp.concatenate([mine, hop_core(other), jnp.zeros((2, n), BF16)], axis=0)
    block = jnp.concatenate([block, lax.ppermute(block, "xl", [(i, i ^ 2) for i in range(16)])], axis=0)
    stack = jnp.concatenate([block, hop_z(block, 4), hop_z(block, 2), hop_z(block, -2)], axis=0)
    r = jnp.arange(48)[:, None]
    s = jnp.arange(64)[None, :]
    slot = s // 16
    j = s % 8
    origin = (z + jnp.where(slot == 1, 4, jnp.where(slot == 2, 6, jnp.where(slot == 3, 2, 0)))) % 8
    row = (origin ^ ((s // 8) % 2)) * 6 + (c ^ (j // 3)) * 3 + j % 3
    order = ((row == r) & (j < 6)).astype(BF16)
    v = jnp.dot(order, stack, preferred_element_type=F32).astype(BF16)
    v = jnp.concatenate(gather4(v, hop_x), axis=0)
    mine = gather4(v, hop_y)
    return mine + [hop_core(u) for u in mine]


def mm(a, b):
    return jnp.dot(a, b, preferred_element_type=F32)


def mm_t(a, b):
    return lax.dot_general(a, b, (((1,), (1,)), ((), ())), preferred_element_type=F32)


def tmm(a, b):
    return lax.dot_general(a, b, (((0,), (0,)), ((), ())), preferred_element_type=F32)


def norm_rows(xf):
    centred = xf - jnp.mean(xf, axis=-1, keepdims=True)
    inv = lax.rsqrt(jnp.mean(centred * centred, axis=-1, keepdims=True) + 1e-6)
    return centred * inv, inv


def row_mask(at_ref, first, group):
    row_id = lax.broadcasted_iota(jnp.int32, (VMAX, D), 0)
    return jnp.concatenate([row_id < at_ref[3 + first + b] for b in range(group)], axis=0)


def core_kernel(*refs):
    at_ref = refs[0]
    pieces = refs[1:9]
    x_ref, cot_ref, gain_ref = refs[9:12]
    w_out, att_out, gp_out, keep_out, send_out = refs[12:17]
    w_ref, nb_ref, go_ref, att_ref, gp_ref, keep_ref, send_ref, w_sems, row_sems, dw_sems = refs[17:]
    step = pl.program_id(0)
    last = pl.num_programs(0) - 1
    factor = HEAD_DIM**-0.5
    core = at_ref[2]

    def weight_copies():
        y, x = at_ref[0], at_ref[1]
        copies = []
        for rel in range(2):
            half = core ^ rel
            for ky in range(4):
                for kx in range(4):
                    row = pl.multiple_of(((y + STEPS[ky]) & 3) * 192 + ((x + STEPS[kx]) & 3) * 48, 16)
                    copies.append(
                        pltpu.make_async_copy(
                            pieces[rel * 4 + ky].at[pl.ds(kx * 48, 48), :],
                            w_ref.at[half, pl.ds(row, 48), :],
                            w_sems.at[len(copies)],
                        )
                    )
        return copies

    whole_w = pltpu.make_async_copy(w_ref, w_out, w_sems.at[32])

    @pl.when(step == 0)
    def _():
        copies = weight_copies()
        for copy in copies:
            copy.start()
        for copy in copies:
            copy.wait()
        whole_w.start()

    normed, _ = norm_rows(x_ref[...].reshape(ROWS, D).astype(F32))
    nb = (normed * gain_ref[...]).astype(BF16)
    mask = row_mask(at_ref, step * GROUP, GROUP)
    go = jnp.where(mask, cot_ref[...].reshape(ROWS, D).astype(F32), 0.0).astype(BF16)
    at = pl.ds(pl.multiple_of(step * ROWS, ROWS), ROWS)
    nb_ref[at, :] = nb
    go_ref[at, :] = go

    qk = mm(nb, w_ref[0]).astype(BF16)
    vv = mm(nb, w_ref[1, :, :HD]).astype(BF16)
    ga = mm(go, w_ref[1, :, HD:]).astype(BF16)
    key_id = lax.broadcasted_iota(jnp.int32, (VMAX, 2 * VMAX), 0)
    lane = lax.broadcasted_iota(jnp.int32, (1, 2 * HEAD_DIM), 1)
    first = jnp.where(lane < HEAD_DIM, 1.0, 0.0)
    m0, m1 = first.astype(BF16), (1.0 - first).astype(BF16)
    f0, f1 = (first * factor).astype(BF16), ((1.0 - first) * factor).astype(BF16)
    pair = lambda a, u, w: jnp.concatenate([a * u, a * w], axis=0)
    stack = lambda a: jnp.concatenate([a[:, :VMAX], a[:, VMAX:]], axis=0)
    for b in range(GROUP):
        live = key_id < at_ref[3 + step * GROUP + b]
        rs = slice(b * VMAX, (b + 1) * VMAX)
        at_b = pl.ds(pl.multiple_of(step * ROWS + b * VMAX, VMAX), VMAX)
        for lo in range(0, HD, 2 * HEAD_DIM):
            hi = lo + 2 * HEAD_DIM
            k = qk[rs, HD + lo : HD + hi]
            v = vv[rs, lo:hi]
            q2 = pair(qk[rs, lo:hi], f0, f1)
            g2 = pair(ga[rs, lo:hi], m0, m1)
            s = jnp.where(live, mm_t(k, q2), -1e30)
            e = jnp.exp(s - jnp.max(s, axis=0, keepdims=True))
            p = e * (1.0 / jnp.sum(e, axis=0, keepdims=True))
            pb = p.astype(BF16)
            dp = mm_t(v, g2)
            ds = (p * (dp - jnp.sum(p * dp, axis=0, keepdims=True))).astype(BF16)
            att_ref[at_b, lo:hi] = tmm(stack(pb), pair(v, m0, m1)).astype(BF16)
            gp_ref[at_b, lo:hi] = tmm(stack(ds), pair(k, f0, f1)).astype(BF16)
            gp_ref[at_b, HD + lo : HD + hi] = mm(ds, q2).astype(BF16)
            gp_ref[at_b, D + lo : D + hi] = mm(pb, g2).astype(BF16)

    def row_copies(i):
        rows = pl.ds(pl.multiple_of(i * ROWS, ROWS), ROWS)
        return (
            pltpu.make_async_copy(att_ref.at[rows, :], att_out.at[rows, :], row_sems.at[0, i]),
            pltpu.make_async_copy(gp_ref.at[rows, :], gp_out.at[rows, :], row_sems.at[1, i]),
        )

    for copy in row_copies(step):
        copy.start()

    @pl.when(step == last)
    def _():
        copies = []
        for i in range(D // 256):
            rr = slice(i * 256, i * 256 + 256)
            gw = tmm(nb_ref[:, rr], gp_ref[...])
            for half, cols, val in (
                (0, slice(0, D), gw[:, :D]),
                (1, slice(0, HD), gw[:, D:]),
                (1, slice(HD, D), tmm(go_ref[:, rr], att_ref[...])),
            ):

                @pl.when(core == half)
                def _():
                    keep_ref[rr, cols] = val

                @pl.when(core != half)
                def _():
                    send_ref[rr, cols] = val.astype(send_ref.dtype)

            copies.append(pltpu.make_async_copy(keep_ref.at[rr, :], keep_out.at[rr, :], dw_sems.at[0, i]))
            copies.append(pltpu.make_async_copy(send_ref.at[rr, :], send_out.at[rr, :], dw_sems.at[1, i]))
            copies[-1].start()
            copies[-2].start()
        whole_w.wait()
        for i in range(BLOCKS // GROUP):
            for copy in row_copies(i):
                copy.wait()
        for copy in copies:
            copy.wait()


def grads_core(at, pieces, tiles, cotan, gain):
    nblock = tiles.shape[0]
    rows = nblock * VMAX
    hbm = pl.BlockSpec(memory_space=pltpu.HBM)
    tile = pl.BlockSpec((GROUP, VMAX, D), lambda i, *_: (i, 0, 0))
    return pl.pallas_call(
        core_kernel,
        grid_spec=pltpu.PrefetchScalarGridSpec(
            num_scalar_prefetch=1,
            grid=(nblock // GROUP,),
            in_specs=[hbm] * 8 + [tile, tile, pl.BlockSpec((1, D), lambda i, *_: (0, 0))],
            out_specs=[hbm] * 3 + [pl.BlockSpec(memory_space=pl.ANY)] * 2,
            scratch_shapes=[
                pltpu.VMEM((2, D, D), BF16),
                pltpu.VMEM((rows, D), BF16),
                pltpu.VMEM((rows, D), BF16),
                pltpu.VMEM((rows, HD), BF16),
                pltpu.VMEM((rows, 3 * HD), BF16),
                pltpu.VMEM((D, D), F32),
                pltpu.VMEM((D, D), BF16),
                pltpu.SemaphoreType.DMA((33,)),
                pltpu.SemaphoreType.DMA((2, nblock // GROUP)),
                pltpu.SemaphoreType.DMA((2, D // 256)),
            ],
        ),
        out_shape=[
            pltpu.HBM((2, D, D), BF16),
            pltpu.HBM((rows, HD), BF16),
            pltpu.HBM((rows, 3 * HD), BF16),
            jax.ShapeDtypeStruct((D, D), F32),
            jax.ShapeDtypeStruct((D, D), BF16),
        ],
        compiler_params=pltpu.CompilerParams(
            dimension_semantics=("arbitrary",), vmem_limit_bytes=CORE_MIB * 1024 * 1024
        ),
        cost_estimate=pl.CostEstimate(flops=20_000_000_000, bytes_accessed=18_000_000, transcendentals=1_200_000),
    )(at, *pieces, tiles, cotan, gain)


def rows_kernel(first, at_ref, w_ref, att_ref, gp_ref, x_ref, cot_ref, gain_ref, *rest):
    enc_ref, gin_ref = rest[-2:]
    gain = gain_ref[...]
    xf = x_ref[...].reshape(TAIL * VMAX, D).astype(F32)
    normed, inv = norm_rows(xf)
    mask = row_mask(at_ref, (first + pl.program_id(0)) * TAIL, TAIL)
    enc = xf + mm_t(att_ref[...], w_ref[1, :, HD:])
    enc_ref[...] = jnp.where(mask, enc, 0.0).astype(BF16).reshape(TAIL, VMAX, D)
    gp = gp_ref[...]
    gn = (mm_t(gp[:, :D], w_ref[0]) + mm_t(gp[:, D:], w_ref[1, :, :HD])) * gain
    gl = inv * (
        gn - jnp.mean(gn, axis=-1, keepdims=True) - normed * jnp.mean(gn * normed, axis=-1, keepdims=True)
    )
    gin = cot_ref[...].reshape(TAIL * VMAX, D).astype(F32) + gl
    gin_ref[...] = jnp.where(mask, gin, 0.0).astype(BF16).reshape(TAIL, VMAX, D)


def rows_part(first, count, at, w, att, gp, tiles, cotan, gain, done):
    tile = pl.BlockSpec((TAIL, VMAX, D), lambda i, *_: (i + first, 0, 0))
    flat = lambda cols: pl.BlockSpec((TAIL * VMAX, cols), lambda i, *_: (i + first, 0))
    return pl.pallas_call(
        functools.partial(rows_kernel, first),
        grid_spec=pltpu.PrefetchScalarGridSpec(
            num_scalar_prefetch=1,
            grid=(count,),
            in_specs=[
                pl.BlockSpec((2, D, D), lambda i, *_: (0, 0, 0), pipeline_mode=pl.Buffered(1)),
                flat(HD),
                flat(3 * HD),
                tile,
                tile,
                pl.BlockSpec((1, D), lambda i, *_: (0, 0)),
            ]
            + [pl.BlockSpec(memory_space=pl.ANY)] * len(done),
            out_specs=[tile, tile],
        ),
        out_shape=[jax.ShapeDtypeStruct(tiles.shape, BF16)] * 2,
        input_output_aliases={7 + i: i for i in range(len(done))},
        compiler_params=pltpu.CompilerParams(
            dimension_semantics=("arbitrary",), vmem_limit_bytes=TAIL_MIB * 1024 * 1024
        ),
        cost_estimate=pl.CostEstimate(
            flops=count * 650_000_000, bytes_accessed=count * 2_500_000, transcendentals=1000
        ),
    )(at, w, att, gp, tiles, cotan, gain, *done)


def small_call(kernel, at, args, outs):
    smem = [] if at is None else [pl.BlockSpec(memory_space=pltpu.SMEM)]
    vmem = pl.BlockSpec(memory_space=pltpu.VMEM)
    size = sum(a.size * a.dtype.itemsize for a in args)
    return pl.pallas_call(
        kernel,
        in_specs=smem + [vmem] * len(args),
        out_specs=[vmem] * len(outs),
        out_shape=[jax.ShapeDtypeStruct(shape, dtype) for shape, dtype in outs],
        compiler_params=pltpu.CompilerParams(vmem_limit_bytes=12 * 1024 * 1024),
        cost_estimate=pl.CostEstimate(flops=size, bytes_accessed=2 * size, transcendentals=0),
    )(*([] if at is None else [at]), *args)


def cut_kernel(axis, at_ref, own_ref, *refs):
    got, outs = refs[:-4], refs[-4:]
    rows = outs[0].shape[0]
    for k in range(4):
        at = pl.ds(pl.multiple_of(((at_ref[axis] + k) & 3) * rows, rows), rows)
        total = own_ref[at, :]
        for ref in got:
            total = total + ref[at, :].astype(F32)
        outs[k][...] = total.astype(outs[k].dtype)


def cut(at, axis, own, *got):
    rows, n = own.shape[0] // 4, own.shape[1]
    outs = [((rows, n), F32)] + [((rows, n), BF16)] * 3
    return small_call(functools.partial(cut_kernel, axis), at, [own, *got], outs)


def triples_kernel(own_ref, *refs):
    total = own_ref[...]
    for ref in refs[:-1]:
        total = total + ref[...].astype(F32)
    for i in range(16):
        refs[-1][i] = total[3 * i : 3 * i + 3, :]


def finish_kernel(got_ref, qkv_ref, out_ref):
    lo, hi = got_ref[0], got_ref[1]
    for z in range(1, 8):
        lo = lo + got_ref[2 * z]
        hi = hi + got_ref[2 * z + 1]
    qkv_ref[:, :D] = lo
    qkv_ref[:, D:] = hi[:, :HD]
    out_ref[...] = hi[:, HD:]


def scatter_grads(at, keep, send, during):
    own, *out = cut(at, 0, keep, hop_core(send))
    got = [hop_y(out[k - 1], k) for k in (2, 1, 3)]
    extra = during(own)
    got[0], extra = lax.optimization_barrier((got[0], extra))
    own, *out = cut(at, 1, own, *got)
    parts = [own] + [hop_x(out[k - 1], k) for k in (2, 1, 3)]
    n = keep.shape[1]
    (v,) = small_call(triples_kernel, None, parts, [((16, 3, n), F32)])
    got = lax.all_to_all(v, "xl", split_axis=0, concat_axis=0, tiled=True)
    return small_call(finish_kernel, None, [got], [((3, n + n // 2), F32), ((3, n // 2), F32)]), extra


def shards(patches, out_cot, vis_count, w_qkv, w_out, ln_gain):
    y, x, z, c = coords()
    pieces = gather_weights(w_qkv, w_out)
    at = jnp.concatenate([jnp.stack([y, x, c]).astype(jnp.int32), vis_count[0]])
    tiles, cotan, gain = patches[0], out_cot[0], ln_gain[None]
    w, att, gp, keep, send = grads_core(at, pieces, tiles, cotan, gain)

    def during(own):
        late, _ = lax.optimization_barrier((at, own))
        return rows_part(0, HEAD, late, w, att, gp, tiles, cotan, gain, ())

    (grad_qkv, grad_out), out = scatter_grads(at, keep, send, during)
    enc, gin = rows_part(HEAD, BLOCKS // TAIL - HEAD, at, w, att, gp, tiles, cotan, gain, out)
    return enc[None], gin[None], grad_qkv, grad_out


def solution(mesh):
    return jax.shard_map(
        shards,
        mesh=mesh,
        in_specs=(
            P("il", "xl", None, None),
            P("il", "xl", None, None),
            P("il", "xl"),
            P(("il", "xl"), None),
            P(("il", "xl"), None),
            P(),
        ),
        out_specs=(
            P("il", "xl", None, None),
            P("il", "xl", None, None),
            P(("il", "xl"), None),
            P(("il", "xl"), None),
        ),
        check_vma=False,
    )
```
